128 devices in a mesh: row: 8 (over z, core), col: 16 (over y, x).
Axes of the slice: x: 4, y: 4, z: 4, core: 2. Of those that a mesh axis runs over, the one named last changes fastest.
Arguments:
- right_side: float32 [8, 65536], P(None, ('row', 'col')), may hold values from -30 to 30
- u_factors: bfloat16 [128, 128, 48, 512], P(('row', 'col')), may hold values from -0.078125 to 0.078125
- v_factors: bfloat16 [128, 128, 48, 512], P('row', 'col'), may hold values from -0.25 to 0.25
- ranks: int32 [128, 128], P('row', 'col'), may hold values from 8 to 48
- far_blocks: bfloat16 [16, 512, 65536], P('row', None, 'col'), may hold values from -0.09375 to 0.09375
- block_target: int32 [16, 16], replicated, may hold values from 0 to 127, as said below
- recv_order: int32 [128], replicated, may hold values from 0 to 127, as said below
Outputs:
- densities: float32 [8, 65536], P(None, 'col')
- residual: float32 [8, 65536], P(None, ('row', 'col'))
- far_field: float32 [128, 4096], P(('row', 'col'))
The draws below stay inside these ranges and needn't reach their ends.
Inputs may be any that keep to these rules, and one draw needn't show every extreme that they name: `recv_order`: a permutation of the receiver patches. `block_target`: block (b, c) with b % 2 == 0 lies on device g = (b // 2) * 16 + c; its receiver patch is stored in output rows owned by device (g + 128 / 2) mod 128 if g is even and by device g - 1 if g is odd; the other blocks may name any receiver patch.
All inputs are finite; a program needn't handle non-finite values.
Results may differ from the reference program's by a relative error of at most 0.008.
Values may be sent and summed in bfloat16 or wider, within the bound.
No kernel may reach another device: no remote copies, remote signals or barrier semaphores. Data moves between devices by JAX's collectives and lax.ppermute only.
A program may use at most 128 MiB of HBM per device.

```python
import jax
import jax.numpy as jnp
from jax import lax

PATCH = 512
RMAX = 48
DENS = 8
CP_DEV = 8
FB_DEV = 2
RECV_DEV = 1
ITERS = 2
NP = 128
MP = 128
ORDER = 65536
FBR = 16
RECV = 128
N_COL = 16
DEVICES = 128


def draw_right_side(key, part):
    total_rows = MP * PATCH
    ramp = 1.0 + 2.0 * jnp.arange(total_rows, dtype=jnp.float32) / (total_rows - 1)
    values = jax.random.normal(key, (DENS, total_rows), jnp.float32)
    return jnp.clip(values, -8.0, 8.0) * ramp[None, :]


def shared_routing(key):
    perm_key = jax.random.fold_in(key, 11)
    return jax.random.permutation(perm_key, RECV).astype(jnp.int32)


def draw_recv_order(key, part):
    return shared_routing(key)


def draw_block_target(key, part):
    perm = shared_routing(key)
    slot_key = jax.random.fold_in(key, 23)
    first_key = jax.random.fold_in(key, 37)
    second_key = jax.random.fold_in(key, 41)
    block_rows = jnp.arange(FBR, dtype=jnp.int32)[:, None]
    col_index = jnp.arange(N_COL, dtype=jnp.int32)[None, :]
    device = block_rows // FB_DEV * N_COL + col_index
    within = block_rows % FB_DEV + 0 * col_index
    partner = jnp.where(device % 2 == 0, (device + DEVICES // 2) % DEVICES, device - 1)
    slot = jax.random.randint(slot_key, (FBR, N_COL), 0, RECV_DEV, dtype=jnp.int32)
    first_pos = partner * RECV_DEV + slot
    draw_one = jax.random.randint(first_key, (FBR, N_COL), 0, RECV, dtype=jnp.int32)
    draw_two = jax.random.randint(second_key, (FBR, N_COL), 0, RECV, dtype=jnp.int32)
    other_pos = jnp.minimum(draw_one, draw_two)
    position = jnp.where(within == 0, first_pos, other_pos).astype(jnp.int32)
    return perm[position]


def place_ends(array, stream_key, low, largest):
    dims = array.shape
    index_at = [jax.random.randint(jax.random.fold_in(stream_key, axis), (), 0, dims[axis]) for axis in range(len(dims))]
    array = array.at[tuple(index_at)].set(low)
    longest = dims.index(max(dims))
    index_at[longest] = (index_at[longest] + 1) % dims[longest]
    return array.at[tuple(index_at)].set(largest)


def block_scale(stream_key, shape, cuts, least, top_value):
    factor_of, own = 1.0, jax.random.fold_in(stream_key, 6)
    for axis_at, parts in cuts:
        draws = jnp.exp(jax.random.uniform(jax.random.fold_in(own, axis_at), (parts,), jnp.float32, least / len(cuts), top_value / len(cuts)))
        factor_of = factor_of * jnp.repeat(draws, shape[axis_at] // parts).reshape([-1 if axis == axis_at else 1 for axis in range(len(shape))])
    return factor_of


def normal_values(rng, shape, scale, limit, cuts=(), kind=jnp.bfloat16):
    values = scale * jax.random.normal(rng, shape, jnp.float32)
    if cuts:
        values = values * block_scale(rng, shape, cuts, -0.22, 0.18)
    return jnp.clip(values, -limit, limit).astype(kind)


def setup_inputs(seed: int = 0) -> dict:
    streams_of = jax.random.split(jax.random.key(seed), 8)
    return {
        "right_side": draw_right_side(jax.random.fold_in(streams_of[7], 71), 0),
        "u_factors": normal_values(streams_of[1], (MP, NP, RMAX, PATCH), (NP * RMAX) ** -0.5, 0.078125, ((0, 128),)),
        "v_factors": normal_values(streams_of[2], (MP, NP, RMAX, PATCH), PATCH ** -0.5, 0.25, ((0, 8), (1, 16))),
        "ranks": place_ends(jax.random.randint(streams_of[3], (MP, NP), RMAX // 6, RMAX + 1), jax.random.fold_in(streams_of[3], 1), RMAX // 6, RMAX).astype(jnp.int32),
        "far_blocks": normal_values(streams_of[4], (FBR, PATCH, ORDER), (CP_DEV * PATCH) ** -0.5, 0.09375, ((0, 8), (2, 16))),
        "block_target": draw_block_target(jax.random.fold_in(streams_of[7], 71), 0),
        "recv_order": draw_recv_order(jax.random.fold_in(streams_of[7], 71), 0),
    }


def reference(right_side, u_factors, v_factors, ranks, far_blocks, block_target, recv_order):
    slot_index = jnp.arange(RMAX, dtype=jnp.int32)
    kept = (slot_index[None, None, :, None] < ranks[:, :, None, None]).astype(jnp.float32)

    def adjoint(residual):
        res_bf = residual.astype(jnp.bfloat16).reshape(DENS, MP, PATCH).transpose(1, 0, 2)

        def accumulate(running, row_items):
            u_row, v_row, kept_row, res_row = row_items
            back_coef = jnp.einsum('jsp,dp->jsd', u_row.astype(jnp.float32), res_row.astype(jnp.float32))
            back_coef = back_coef.astype(jnp.bfloat16) * kept_row.astype(jnp.bfloat16)
            term = jnp.einsum('jsp,jsd->djp', v_row.astype(jnp.float32), back_coef.astype(jnp.float32))
            return running + term, None

        start_sum = jnp.zeros((DENS, NP, PATCH), jnp.float32)
        running, _ = lax.scan(accumulate, start_sum, (u_factors, v_factors, kept, res_bf))
        return running.reshape(DENS, NP * PATCH)

    def forward(grad):
        grad_bf = grad.astype(jnp.bfloat16).astype(jnp.float32).reshape(DENS, NP, PATCH)

        def one_row(row_items):
            u_row, v_row, kept_row = row_items
            coefficients = jnp.einsum('jsp,djp->jsd', v_row.astype(jnp.float32), grad_bf) * kept_row
            coefficients = coefficients.astype(jnp.bfloat16).astype(jnp.float32)
            return jnp.einsum('jsp,jsd->dp', u_row.astype(jnp.float32), coefficients)

        image = lax.map(one_row, (u_factors, v_factors, kept))
        return image.transpose(1, 0, 2).reshape(DENS, MP * PATCH)

    residual = right_side
    densities = jnp.zeros((DENS, NP * PATCH), jnp.float32)
    for iteration in range(ITERS):
        grad = adjoint(residual)
        grad_sq = jnp.sum(grad * grad, axis=1)
        image = forward(grad)
        image_sq = jnp.sum(image * image, axis=1)
        step_size = grad_sq / (image_sq + 1e-6)
        densities = densities + step_size[:, None] * grad
        residual = residual - step_size[:, None] * image

    x_groups = densities.astype(jnp.bfloat16).astype(jnp.float32).reshape(DENS, N_COL, CP_DEV * PATCH)

    def block_row(far_row):
        far_split = far_row.astype(jnp.float32).reshape(PATCH, N_COL, CP_DEV * PATCH)
        field = jnp.einsum('pcn,dcn->cdp', far_split, x_groups)
        return field.reshape(N_COL, DENS * PATCH)

    block_field = lax.map(block_row, far_blocks).reshape(FBR * N_COL, DENS * PATCH)
    onehot = (block_target.reshape(-1)[:, None] == recv_order[None, :]).astype(jnp.float32)
    far_field = jnp.dot(onehot.T, block_field, preferred_element_type=jnp.float32, precision=lax.Precision.HIGHEST)
    return densities, residual, far_field
```

```python
import jax
import jax.numpy as jnp
from jax import lax
from jax.experimental import pallas as pl
from jax.experimental.pallas import tpu as pltpu
from jax.sharding import PartitionSpec as P

F32, BF16 = jnp.float32, jnp.bfloat16
MIB = 1 << 20


def dot_nt(a, b):
    return lax.dot_general(a, b, (((1,), (1,)), ((), ())), preferred_element_type=F32)


def dot_nn(a, b):
    return lax.dot_general(a, b, (((1,), (0,)), ((), ())), preferred_element_type=F32)


def spread(value):
    high = value.astype(BF16).astype(F32)
    rest = value - high
    mid = rest.astype(BF16).astype(F32)
    low = rest - mid
    lane = lax.broadcasted_iota(jnp.int32, (value.shape[0], 128), 1)
    zero = jnp.zeros((value.shape[0], 128), F32)
    return jnp.where(
        lane == 0, high, jnp.where(lane == 1, mid, jnp.where(lane == 2, low, zero))
    ).astype(BF16)


def gather_sum(ref, low, width):
    total = ref[0, :, low : low + width].astype(F32)
    for source in range(1, ref.shape[0]):
        total = total + ref[source, :, low : low + width].astype(F32)
    return total


def call(kernel, outs, args, smem=(), scratch=(), limit=8):
    vm = pl.BlockSpec(memory_space=pltpu.VMEM)
    sm = pl.BlockSpec(memory_space=pltpu.SMEM)
    return pl.pallas_call(
        kernel,
        out_shape=tuple(jax.ShapeDtypeStruct(s, d) for s, d in outs),
        in_specs=[sm if at in smem else vm for at in range(len(args))],
        out_specs=tuple(vm for _ in outs),
        scratch_shapes=list(scratch),
        compiler_params=pltpu.CompilerParams(vmem_limit_bytes=limit * MIB),
        name=kernel.__name__,
    )(*args)


def per_device(right_side, u_factors, v_factors, ranks, far_blocks, block_target, recv_order):
    dens = right_side.shape[0]
    all_cols, slots, patch = u_factors.shape[1:]
    rows, cols = v_factors.shape[:2]
    peers = all_cols // cols
    wide = cols * slots
    n_row = lax.axis_size("row")
    tall = cols * dens
    blocks = far_blocks.shape[0]

    def in_vmem(x):
        return pltpu.with_memory_space_constraint(x, pltpu.VMEM)

    u_all = in_vmem(u_factors.reshape(all_cols * slots, patch))
    v_all = in_vmem(v_factors.reshape(rows * wide, patch))
    far_all = in_vmem(far_blocks)
    bound = jnp.repeat(
        (ranks + slots * jnp.arange(cols, dtype=jnp.int32)[None, :]).T, dens, axis=0
    )

    def kept_lanes(bound_ref, row_patch):
        lane = lax.broadcasted_iota(jnp.int32, (tall, wide), 1)
        first = lax.broadcasted_iota(jnp.int32, (tall, wide), 0) // dens * slots
        return (lane >= first) & (lane < bound_ref[:, row_patch : row_patch + 1])

    def back_kernel(res_ref, u_ref, out_ref):
        back = dot_nt(res_ref[...].astype(BF16), u_ref[...])
        for peer in range(peers):
            out_ref[peer] = back[:, peer * wide : (peer + 1) * wide].astype(BF16)

    def fill_left(in_ref, bound_ref, left_ref):
        for i in range(rows):
            piece = in_ref[i, :, 0:wide].astype(F32)
            stacked = jnp.concatenate([piece] * cols, axis=0)
            left_ref[:, i * wide : (i + 1) * wide] = jnp.where(
                kept_lanes(bound_ref, i), stacked, 0.0
            ).astype(BF16)

    def grad_kernel(in_ref, bound_ref, v_ref, out_ref, left_ref):
        fill_left(in_ref, bound_ref, left_ref)
        out_ref[...] = dot_nn(left_ref[...], v_ref[...])

    def grad_norm_kernel(in_ref, bound_ref, v_ref, out_ref, left_ref):
        fill_left(in_ref, bound_ref, left_ref)
        out_ref[0:tall, :] = dot_nn(left_ref[...], v_ref[...])
        norm = jnp.sum(gather_sum(in_ref, wide, 128), axis=1, keepdims=True)
        out_ref[tall : tall + dens, :] = jnp.broadcast_to(norm, (dens, patch))

    def coefficients(grad, bound_ref, v_ref, out_ref):
        half = grad.astype(BF16)
        for i in range(0, rows, 2):
            both = dot_nt(half, v_ref[i * wide : (i + 2) * wide, :])
            for k in range(2):
                part = jnp.where(
                    kept_lanes(bound_ref, i + k), both[:, k * wide : (k + 1) * wide], 0.0
                )
                total = part[0:dens]
                for j in range(1, cols):
                    total = total + part[j * dens : (j + 1) * dens]
                out_ref[i + k, :, 0:wide] = total.astype(BF16)

    def norm_of(grad):
        line = jnp.sum(grad * grad, axis=1, keepdims=True)
        total = line[0:dens]
        for j in range(1, line.shape[0] // dens):
            total = total + line[j * dens : (j + 1) * dens]
        return total

    def coef_kernel(p0_ref, p2_ref, p4_ref, p6_ref, bound_ref, v_ref, out_ref, grad_ref):
        grad = (p0_ref[...].astype(F32) + p2_ref[...].astype(F32)) + (
            p4_ref[...].astype(F32) + p6_ref[...].astype(F32)
        )
        grad_ref[...] = grad
        coefficients(grad, bound_ref, v_ref, out_ref)
        mine = spread(norm_of(grad))
        for i in range(rows):
            out_ref[i, :, wide : wide + 128] = mine

    def image_of(in_ref, u_ref):
        left = jnp.concatenate([in_ref[c, :, 0:wide] for c in range(peers)], axis=1)
        return dot_nn(left, u_ref[...])

    def image_back_kernel(in_ref, u_ref, image_ref, gsq_ref, out_ref):
        image = image_of(in_ref, u_ref)
        image_ref[...] = image
        gsq_ref[...] = jnp.broadcast_to(
            jnp.sum(gather_sum(in_ref, wide, 128), axis=1, keepdims=True), (dens, 128)
        )
        high = image.astype(BF16)
        low = (image - high.astype(F32)).astype(BF16)
        both = dot_nt(jnp.concatenate([high, low], axis=0), u_ref[...])
        back = both[0:dens] + both[dens : 2 * dens]
        mine = spread(norm_of(image))
        for peer in range(peers):
            out_ref[peer, :, 0:wide] = back[:, peer * wide : (peer + 1) * wide].astype(BF16)
            out_ref[peer, :, wide : wide + 128] = mine

    far_low = wide + 128

    def coef_far_kernel(
        p0_ref, p2_ref, p4_ref, p6_ref, grad_ref, gsq_ref, bound_ref, v_ref, far_ref,
        out_ref, first_ref, second_ref, step_ref, even_ref,
    ):
        wave = (p0_ref[...].astype(F32) + p2_ref[...].astype(F32)) + (
            p4_ref[...].astype(F32) + p6_ref[...].astype(F32)
        )
        isq = jnp.sum(wave[tall : tall + dens, 0:128], axis=1, keepdims=True)
        step = gsq_ref[:, 0:1] / (isq + 1e-6)
        step_ref[...] = jnp.broadcast_to(step, (dens, 128))
        steps = jnp.concatenate([step] * cols, axis=0)
        first = steps * grad_ref[...]
        second = grad_ref[...] - steps * wave[0:tall]
        first_ref[...] = first
        second_ref[...] = second
        coefficients(second, bound_ref, v_ref, out_ref)
        mine = spread(norm_of(second))
        first_row = jnp.concatenate([first[j * dens : (j + 1) * dens] for j in range(cols)], axis=1)
        second_row = jnp.concatenate(
            [second[j * dens : (j + 1) * dens] for j in range(cols)], axis=1
        )
        left = jnp.concatenate([first_row, second_row], axis=0).astype(BF16)
        even = dot_nt(left, far_ref[0])
        odd = dot_nt(left, far_ref[1])
        even_ref[...] = jnp.concatenate([even[0:dens], even[dens : 2 * dens]], axis=1).astype(BF16)
        send = jnp.concatenate([odd[0:dens], odd[dens : 2 * dens]], axis=1).astype(BF16)
        for i in range(rows):
            out_ref[i, :, wide : wide + 128] = mine
            out_ref[i, :, far_low : far_low + 2 * patch] = send

    def image_far_kernel(route_ref, even_ref, in_ref, u_ref, image_ref, gsq_ref, out_ref):
        image = image_of(in_ref, u_ref)
        image_ref[...] = image
        gsq_ref[...] = jnp.broadcast_to(
            jnp.sum(gather_sum(in_ref, wide, 128), axis=1, keepdims=True), (dens, 128)
        )
        mine = spread(norm_of(image))
        for target in range(n_row):
            total = even_ref[...].astype(F32) * route_ref[target, peers]
            for source in range(peers):
                total = total + in_ref[source, :, far_low : far_low + 2 * patch].astype(
                    F32
                ) * route_ref[target, source]
            out_ref[target, :, 0 : 2 * patch] = total.astype(BF16)
            out_ref[target, :, 2 * patch : 2 * patch + 128] = mine

    def relay_kernel(in_ref, out_ref):
        mine = spread(jnp.sum(gather_sum(in_ref, 2 * patch, 128), axis=1, keepdims=True))
        for peer in range(peers):
            out_ref[peer] = mine

    def finish_kernel(
        norm_ref, gsq_ref, first_ref, second_ref, res_ref, image1_ref, image2_ref, step_ref,
        far_ref, side_ref, dens_ref, out_res_ref, out_far_ref,
    ):
        isq = jnp.sum(gather_sum(norm_ref, 0, 128), axis=1, keepdims=True)
        step = gsq_ref[:, 0:1] / (isq + 1e-6)
        for j in range(cols):
            at = slice(j * dens, (j + 1) * dens)
            dens_ref[:, j * patch : (j + 1) * patch] = first_ref[at] + step * second_ref[at]
        out_res_ref[...] = (
            res_ref[...] - step_ref[:, 0:1] * image1_ref[...] - step * image2_ref[...]
        )
        both = gather_sum(far_ref, 0, 2 * patch) + side_ref[...].astype(F32)
        field = both[:, 0:patch] + step * both[:, patch : 2 * patch]
        for d in range(dens):
            out_far_ref[:, d * patch : (d + 1) * patch] = field[d : d + 1]

    def over_rows(part):
        pair = part + lax.ppermute(part, "row", [(i, i ^ 1) for i in range(n_row)])
        if pair.shape[0] > tall:
            high = lax.reduce_precision(pair, 8, 7)
            rest = pair - high
            mid = lax.reduce_precision(rest, 8, 7)
            row = lax.broadcasted_iota(jnp.int32, pair.shape, 0)
            lane = lax.broadcasted_iota(jnp.int32, pair.shape, 1)
            terms = jnp.where(
                lane == 0, high, jnp.where(lane == 1, mid, jnp.where(lane == 2, rest - mid, 0.0))
            )
            pair = jnp.where(row < tall, pair, terms)
        half = lax.optimization_barrier(pair.astype(BF16))
        return [half] + [
            lax.ppermute(half, "row", [(i, i ^ k) for i in range(n_row)]) for k in (2, 4, 6)
        ]

    def over_col(x):
        return lax.all_to_all(x, "col", split_axis=0, concat_axis=0, tiled=True)

    me_row, me_col = lax.axis_index("row"), lax.axis_index("col")
    odd_targets = lax.dynamic_slice(block_target, (me_row * blocks + 1, 0), (1, peers))
    my_order = lax.dynamic_slice(recv_order.reshape(n_row, peers), (0, me_col), (n_row, 1))
    partner = (jnp.arange(n_row) == (me_row + n_row // 2) % n_row) & (me_col % 2 == 0)
    route = jnp.concatenate([my_order == odd_targets, partner[:, None]], axis=1).astype(F32)

    left_scratch = (pltpu.VMEM((tall, rows * wide), BF16),)
    (sent,) = call(back_kernel, [((peers, dens, wide), BF16)], [right_side, u_all])
    (part,) = call(
        grad_kernel, [((tall, patch), F32)], [over_col(sent), bound, v_all], scratch=left_scratch
    )
    sent, grad = call(
        coef_kernel,
        [((rows, dens, wide + 128), BF16), ((tall, patch), F32)],
        over_rows(part) + [bound, v_all],
    )
    image1, gsq1, sent = call(
        image_back_kernel,
        [((dens, patch), F32), ((dens, 128), F32), ((peers, dens, wide + 128), BF16)],
        [over_col(sent), u_all],
    )
    (part,) = call(
        grad_norm_kernel,
        [((tall + dens, patch), F32)],
        [over_col(sent), bound, v_all],
        scratch=left_scratch,
    )
    sent, first, second, step1, even = call(
        coef_far_kernel,
        [
            ((rows, dens, far_low + 2 * patch), BF16),
            ((tall, patch), F32),
            ((tall, patch), F32),
            ((dens, 128), F32),
            ((dens, 2 * patch), BF16),
        ],
        over_rows(part) + [grad, gsq1, bound, v_all, far_all],
    )
    side = lax.ppermute(even, "col", [(c, c - 1) for c in range(1, peers, 2)])
    image2, gsq2, sent = call(
        image_far_kernel,
        [((dens, patch), F32), ((dens, 128), F32), ((n_row, dens, 2 * patch + 128), BF16)],
        [route, even, over_col(sent), u_all],
        smem=(0,),
    )
    far_in = lax.all_to_all(sent, "row", split_axis=0, concat_axis=0, tiled=True)
    (relayed,) = call(relay_kernel, [((peers, dens, 128), BF16)], [far_in])
    densities, residual, far_field = call(
        finish_kernel,
        [((dens, cols * patch), F32), ((dens, patch), F32), ((1, dens * patch), F32)],
        [over_col(relayed), gsq2, first, second, right_side, image1, image2, step1, far_in, side],
    )
    return densities, residual, far_field


def solution(mesh):
    return jax.shard_map(
        per_device,
        mesh=mesh,
        in_specs=(
            P(None, ("row", "col")),
            P(("row", "col"), None, None, None),
            P("row", "col", None, None),
            P("row", "col"),
            P("row", None, "col"),
            P(),
            P(),
        ),
        out_specs=(P(None, "col"), P(None, ("row", "col")), P(("row", "col"), None)),
        check_vma=False,
    )
```

```python
import jax
import jax.numpy as jnp
from jax import lax
from jax.experimental import pallas as pl
from jax.experimental.pallas import tpu as pltpu
from jax.sharding import PartitionSpec as P

F32, BF16 = jnp.float32, jnp.bfloat16
MIB = 1 << 20


def dot_nt(a, b):
    return lax.dot_general(a, b, (((1,), (1,)), ((), ())), preferred_element_type=F32)


def dot_nn(a, b):
    return lax.dot_general(a, b, (((1,), (0,)), ((), ())), preferred_element_type=F32)


def spread(value):
    high = value.astype(BF16).astype(F32)
    rest = value - high
    mid = rest.astype(BF16).astype(F32)
    low = rest - mid
    lane = lax.broadcasted_iota(jnp.int32, (value.shape[0], 128), 1)
    zero = jnp.zeros((value.shape[0], 128), F32)
    return jnp.where(
        lane == 0, high, jnp.where(lane == 1, mid, jnp.where(lane == 2, low, zero))
    ).astype(BF16)


def gather_sum(ref, low, width):
    total = ref[0, :, low : low + width].astype(F32)
    for source in range(1, ref.shape[0]):
        total = total + ref[source, :, low : low + width].astype(F32)
    return total


def call(kernel, outs, args, smem=(), hbm=(), keep=(), scratch=(), limit=8):
    vm = pl.BlockSpec(memory_space=pltpu.VMEM)
    sm = pl.BlockSpec(memory_space=pltpu.SMEM)
    far_away = pl.BlockSpec(memory_space=pltpu.HBM)
    return pl.pallas_call(
        kernel,
        out_shape=tuple(
            pltpu.VMEM(s, d) if at in keep else jax.ShapeDtypeStruct(s, d)
            for at, (s, d) in enumerate(outs)
        ),
        in_specs=[
            sm if at in smem else far_away if at in hbm else vm for at in range(len(args))
        ],
        out_specs=tuple(vm for _ in outs),
        scratch_shapes=list(scratch),
        compiler_params=pltpu.CompilerParams(vmem_limit_bytes=limit * MIB),
        name=kernel.__name__,
    )(*args)


def per_device(right_side, u_factors, v_factors, ranks, far_blocks, block_target, recv_order):
    dens = right_side.shape[0]
    all_cols, slots, patch = u_factors.shape[1:]
    rows, cols = v_factors.shape[:2]
    peers = all_cols // cols
    wide = cols * slots
    n_row = lax.axis_size("row")
    devices = n_row * peers
    tall = cols * dens
    blocks = far_blocks.shape[0]

    u_flat = pltpu.with_memory_space_constraint(
        u_factors.reshape(all_cols * slots, patch), pltpu.HBM
    )
    v_all = pltpu.with_memory_space_constraint(v_factors.reshape(rows * wide, patch), pltpu.VMEM)
    far_all = pltpu.with_memory_space_constraint(far_blocks, pltpu.VMEM)
    parts = 8
    def kept_lanes(bound_ref, row_patch):
        lane = lax.broadcasted_iota(jnp.int32, (tall, wide), 1)
        first = lax.broadcasted_iota(jnp.int32, (tall, wide), 0) // dens * slots
        at = lane - first
        return (at >= 0) & (at < bound_ref[:, row_patch : row_patch + 1])

    def back_kernel(res_hbm, u_hbm, out_ref, u_ref, res_ref, sems):
        share = u_flat.shape[0] // parts
        each = peers // parts
        copies = [pltpu.make_async_copy(res_hbm, res_ref, sems.at[parts])]
        for part in range(parts):
            at = pl.ds(part * share, share)
            copies.append(pltpu.make_async_copy(u_hbm.at[at], u_ref.at[at], sems.at[part]))
        for copy in copies:
            copy.start()
        copies[0].wait()
        half = res_ref[...].astype(BF16)
        for part in range(parts):
            copies[part + 1].wait()
            back = dot_nt(half, u_ref[part * share : (part + 1) * share, :])
            for k in range(each):
                out_ref[part * each + k] = back[:, k * wide : (k + 1) * wide].astype(BF16)

    def fill_left(in_ref, bound_ref, left_ref):
        for i in range(rows):
            piece = in_ref[i, :, 0:wide].astype(F32)
            stacked = jnp.concatenate([piece] * cols, axis=0)
            left_ref[:, i * wide : (i + 1) * wide] = jnp.where(
                kept_lanes(bound_ref, i), stacked, 0.0
            ).astype(BF16)

    def grad_kernel(in_ref, bound_ref, v_ref, out_ref, left_ref):
        fill_left(in_ref, bound_ref, left_ref)
        out_ref[...] = dot_nn(left_ref[...], v_ref[...])

    def grad_norm_kernel(in_ref, bound_ref, v_ref, out_ref, left_ref):
        fill_left(in_ref, bound_ref, left_ref)
        out_ref[0:tall, :] = dot_nn(left_ref[...], v_ref[...])
        norm = jnp.sum(gather_sum(in_ref, wide, 128), axis=1, keepdims=True)
        out_ref[tall : tall + dens, :] = jnp.broadcast_to(norm, (dens, patch))

    def coefficients(grad, bound_ref, v_ref, out_ref):
        half = grad.astype(BF16)
        for i in range(0, rows, 2):
            both = dot_nt(half, v_ref[i * wide : (i + 2) * wide, :])
            for k in range(2):
                part = jnp.where(
                    kept_lanes(bound_ref, i + k), both[:, k * wide : (k + 1) * wide], 0.0
                )
                total = part[0:dens]
                for j in range(1, cols):
                    total = total + part[j * dens : (j + 1) * dens]
                out_ref[i + k, :, 0:wide] = total.astype(BF16)

    def norm_of(grad):
        line = jnp.sum(grad * grad, axis=1, keepdims=True)
        total = line[0:dens]
        for j in range(1, line.shape[0] // dens):
            total = total + line[j * dens : (j + 1) * dens]
        return total

    def coef_kernel(p0_ref, p2_ref, p4_ref, p6_ref, bound_ref, v_ref, out_ref, grad_ref):
        grad = (p0_ref[...].astype(F32) + p2_ref[...].astype(F32)) + (
            p4_ref[...].astype(F32) + p6_ref[...].astype(F32)
        )
        grad_ref[...] = grad
        coefficients(grad, bound_ref, v_ref, out_ref)
        mine = spread(norm_of(grad))
        for i in range(rows):
            out_ref[i, :, wide : wide + 128] = mine

    def image_of(in_ref, u_ref):
        left = jnp.concatenate([in_ref[c, :, 0:wide] for c in range(peers)], axis=1)
        return dot_nn(left, u_ref[...])

    def image_back_kernel(in_ref, u_ref, image_ref, gsq_ref, out_ref):
        image = image_of(in_ref, u_ref)
        image_ref[...] = image
        gsq_ref[...] = jnp.broadcast_to(
            jnp.sum(gather_sum(in_ref, wide, 128), axis=1, keepdims=True), (dens, 128)
        )
        high = image.astype(BF16)
        low = (image - high.astype(F32)).astype(BF16)
        both = dot_nt(jnp.concatenate([high, low], axis=0), u_ref[...])
        back = both[0:dens] + both[dens : 2 * dens]
        mine = spread(norm_of(image))
        for peer in range(peers):
            out_ref[peer, :, 0:wide] = back[:, peer * wide : (peer + 1) * wide].astype(BF16)
            out_ref[peer, :, wide : wide + 128] = mine

    far_low = wide + 128

    def coef_far_kernel(
        p0_ref, p2_ref, p4_ref, p6_ref, grad_ref, gsq_ref, bound_ref, v_ref, far_ref,
        out_ref, first_ref, second_ref, step_ref, even_ref,
    ):
        wave = (p0_ref[...].astype(F32) + p2_ref[...].astype(F32)) + (
            p4_ref[...].astype(F32) + p6_ref[...].astype(F32)
        )
        isq = jnp.sum(wave[tall : tall + dens, 0:128], axis=1, keepdims=True)
        step = gsq_ref[:, 0:1] / (isq + 1e-6)
        step_ref[...] = jnp.broadcast_to(step, (dens, 128))
        steps = jnp.concatenate([step] * cols, axis=0)
        first = steps * grad_ref[...]
        second = grad_ref[...] - steps * wave[0:tall]
        first_ref[...] = first
        second_ref[...] = second
        coefficients(second, bound_ref, v_ref, out_ref)
        mine = spread(norm_of(second))
        lines = [
            jnp.concatenate([x[j * dens : (j + 1) * dens] for j in range(cols)], axis=1)
            for x in (first, second)
        ]
        left = jnp.concatenate(lines, axis=0).astype(BF16)
        even = dot_nt(left, far_ref[0])
        odd = dot_nt(left, far_ref[1])
        even_ref[...] = jnp.concatenate([even[0:dens], even[dens : 2 * dens]], axis=1).astype(BF16)
        send = jnp.concatenate([odd[0:dens], odd[dens : 2 * dens]], axis=1).astype(BF16)
        for i in range(rows):
            out_ref[i, :, wide : wide + 128] = mine
            out_ref[i, :, far_low : far_low + 2 * patch] = send

    def image_last_kernel(in_ref, u_ref, image_ref, gsq_ref, out_ref):
        image = image_of(in_ref, u_ref)
        image_ref[...] = image
        gsq_ref[...] = jnp.broadcast_to(
            jnp.sum(gather_sum(in_ref, wide, 128), axis=1, keepdims=True), (dens, 128)
        )
        here = lax.broadcasted_iota(jnp.int32, (dens, 128), 0) == lax.broadcasted_iota(
            jnp.int32, (dens, 128), 1
        )
        line = jnp.sum(jnp.where(here, norm_of(image), 0.0), axis=0, keepdims=True)
        for peer in range(devices):
            out_ref[peer] = line

    def route_kernel(target_ref, order_ref, even_ref, in_ref, keep_ref, give_ref):
        row, col = lax.axis_index("row"), lax.axis_index("col")
        for m in range(n_row):
            mine = order_ref[lax.bitwise_xor(row, m) * peers + col]
            total = jnp.zeros((dens, 2 * patch), F32)
            if m == n_row // 2:
                total = even_ref[...].astype(F32) * jnp.where(col % 2 == 0, 1.0, 0.0)
            for source in range(peers):
                hit = jnp.where(target_ref[row * blocks + 1, source] == mine, 1.0, 0.0)
                piece = in_ref[source, :, far_low : far_low + 2 * patch].astype(F32)
                total = total + piece * hit
            out_ref = keep_ref if m % 2 == 0 else give_ref
            out_ref[m // 2] = total.astype(BF16)

    def pair_kernel(own_ref, other_ref, out_ref):
        out_ref[0:tall, :] = (own_ref[0:tall] + other_ref[0:tall]).astype(BF16)
        low = slice(tall, tall + dens)
        out_ref[low, 0:128] = spread(own_ref[low, 0:1] + other_ref[low, 0:1])
        out_ref[low, 128:patch] = jnp.zeros((dens, patch - 128), BF16)

    def finish_kernel(
        norm_ref, gsq_ref, first_ref, second_ref, res_ref, image1_ref, image2_ref, step_ref,
        f0_ref, f2_ref, f4_ref, f6_ref, side_ref, dens_ref, out_res_ref, out_far_ref,
    ):
        line = norm_ref[0]
        for source in range(1, devices):
            line = line + norm_ref[source]
        here = lax.broadcasted_iota(jnp.int32, (dens, 128), 0) == lax.broadcasted_iota(
            jnp.int32, (dens, 128), 1
        )
        isq = jnp.sum(jnp.where(here, line, 0.0), axis=1, keepdims=True)
        step = gsq_ref[:, 0:1] / (isq + 1e-6)
        for j in range(cols):
            at = slice(j * dens, (j + 1) * dens)
            dens_ref[:, j * patch : (j + 1) * patch] = first_ref[at] + step * second_ref[at]
        out_res_ref[...] = (
            res_ref[...] - step_ref[:, 0:1] * image1_ref[...] - step * image2_ref[...]
        )
        both = side_ref[...].astype(F32)
        for ref in (f0_ref, f2_ref, f4_ref, f6_ref):
            both = both + ref[...].astype(F32)
        field = both[:, 0:patch] + step * both[:, patch : 2 * patch]
        for d in range(dens):
            out_far_ref[:, d * patch : (d + 1) * patch] = field[d : d + 1]

    def row_shift(x, k):
        return lax.ppermute(x, "row", [(i, i ^ k) for i in range(n_row)])

    def over_rows(part):
        other = row_shift(part, 1)
        if part.shape[0] > tall:
            (half,) = call(pair_kernel, [(part.shape, BF16)], [part, other])
        else:
            half = (part + other).astype(BF16)
        half = lax.optimization_barrier(half)
        return [half] + [row_shift(half, k) for k in (2, 4, 6)]

    def over_col(x):
        return lax.all_to_all(x, "col", split_axis=0, concat_axis=0, tiled=True)

    left_scratch = (pltpu.VMEM((tall, rows * wide), BF16),)
    dma = pltpu.SemaphoreType.DMA
    sent, u_all = call(
        back_kernel,
        [((peers, dens, wide), BF16), (u_flat.shape, BF16)],
        [pltpu.with_memory_space_constraint(right_side, pltpu.HBM), u_flat],
        hbm=(0, 1),
        keep=(1,),
        scratch=(pltpu.VMEM((dens, patch), F32), dma((parts + 1,))),
    )
    landed, known = lax.optimization_barrier((over_col(sent), ranks))
    bound = jnp.repeat(known.T, dens, axis=0)
    (part,) = call(
        grad_kernel, [((tall, patch), F32)], [landed, bound, v_all], scratch=left_scratch
    )
    sent, grad = call(
        coef_kernel,
        [((rows, dens, wide + 128), BF16), ((tall, patch), F32)],
        over_rows(part) + [bound, v_all],
    )
    image1, gsq1, sent = call(
        image_back_kernel,
        [((dens, patch), F32), ((dens, 128), F32), ((peers, dens, wide + 128), BF16)],
        [over_col(sent), u_all],
    )
    (part,) = call(
        grad_norm_kernel,
        [((tall + dens, patch), F32)],
        [over_col(sent), bound, v_all],
        scratch=left_scratch,
    )
    sent, first, second, step1, even = call(
        coef_far_kernel,
        [
            ((rows, dens, far_low + 2 * patch), BF16),
            ((tall, patch), F32),
            ((tall, patch), F32),
            ((dens, 128), F32),
            ((dens, 2 * patch), BF16),
        ],
        over_rows(part) + [grad, gsq1, bound, v_all, far_all],
    )
    landed = over_col(sent)
    image2, gsq2, sent = call(
        image_last_kernel,
        [((dens, patch), F32), ((dens, 128), F32), ((devices, 1, 128), F32)],
        [landed, u_all],
    )
    norms = lax.all_to_all(sent, ("row", "col"), split_axis=0, concat_axis=0, tiled=True)
    keep, give = call(
        route_kernel,
        [((n_row // 2, dens, 2 * patch), BF16)] * 2,
        [block_target, recv_order, even, landed],
        smem=(0, 1),
    )
    near = keep + row_shift(give, 1)
    pieces = [near[0]] + [row_shift(near[k], 2 * k) for k in range(1, n_row // 2)]
    side = lax.ppermute(even, "col", [(c, c - 1) for c in range(1, peers, 2)])
    densities, residual, far_field = call(
        finish_kernel,
        [((dens, cols * patch), F32), ((dens, patch), F32), ((1, dens * patch), F32)],
        [norms, gsq2, first, second, right_side, image1, image2, step1] + pieces + [side],
    )
    return densities, residual, far_field


def solution(mesh):
    return jax.shard_map(
        per_device,
        mesh=mesh,
        in_specs=(
            P(None, ("row", "col")),
            P(("row", "col"), None, None, None),
            P("row", "col", None, None),
            P("row", "col"),
            P("row", None, "col"),
            P(),
            P(),
        ),
        out_specs=(P(None, "col"), P(None, ("row", "col")), P(("row", "col"), None)),
        check_vma=False,
    )
```

```python
import jax
import jax.numpy as jnp
from jax import lax
from jax.experimental import pallas as pl
from jax.experimental.pallas import tpu as pltpu
from jax.sharding import PartitionSpec as P


F32, BF16 = jnp.float32, jnp.bfloat16
MIB = 1 << 20


def dot_nt(a, b):
    return lax.dot_general(a, b, (((1,), (1,)), ((), ())), preferred_element_type=F32)


def dot_nn(a, b):
    return lax.dot_general(a, b, (((1,), (0,)), ((), ())), preferred_element_type=F32)


def spread(value):
    high = value.astype(BF16).astype(F32)
    rest = value - high
    mid = rest.astype(BF16).astype(F32)
    low = rest - mid
    lane = lax.broadcasted_iota(jnp.int32, (value.shape[0], 128), 1)
    zero = jnp.zeros((value.shape[0], 128), F32)
    return jnp.where(
        lane == 0, high, jnp.where(lane == 1, mid, jnp.where(lane == 2, low, zero))
    ).astype(BF16)


def gather_sum(ref, low, width):
    total = ref[0, :, low : low + width].astype(F32)
    for source in range(1, ref.shape[0]):
        total = total + ref[source, :, low : low + width].astype(F32)
    return total


def call(kernel, outs, args, smem=(), hbm=(), keep=(), scratch=(), limit=8):
    vm = pl.BlockSpec(memory_space=pltpu.VMEM)
    sm = pl.BlockSpec(memory_space=pltpu.SMEM)
    far_away = pl.BlockSpec(memory_space=pltpu.HBM)
    return pl.pallas_call(
        kernel,
        out_shape=tuple(
            pltpu.VMEM(s, d) if at in keep else jax.ShapeDtypeStruct(s, d)
            for at, (s, d) in enumerate(outs)
        ),
        in_specs=[
            sm if at in smem else far_away if at in hbm else vm for at in range(len(args))
        ],
        out_specs=tuple(vm for _ in outs),
        scratch_shapes=list(scratch),
        compiler_params=pltpu.CompilerParams(vmem_limit_bytes=limit * MIB),
    )(*args)


def per_device(right_side, u_factors, v_factors, ranks, far_blocks, block_target, recv_order):
    dens = right_side.shape[0]
    all_cols, slots, patch = u_factors.shape[1:]
    rows, cols = v_factors.shape[:2]
    peers = all_cols // cols
    wide = cols * slots
    n_row = lax.axis_size("row")
    devices = n_row * peers
    tall = cols * dens
    blocks = far_blocks.shape[0]

    u_flat = pltpu.with_memory_space_constraint(
        u_factors.reshape(all_cols * slots, patch), pltpu.HBM
    )
    far_all = pltpu.with_memory_space_constraint(far_blocks, pltpu.VMEM)
    parts = 8

    def kept_lanes(bound_ref, row_patch):
        lane = lax.broadcasted_iota(jnp.int32, (tall, wide), 1)
        first = lax.broadcasted_iota(jnp.int32, (tall, wide), 0) // dens * slots
        at = lane - first
        return (at >= 0) & (at < bound_ref[:, row_patch : row_patch + 1])

    def back_kernel(res_hbm, u_hbm, out_ref, u_ref, res_ref, sems):
        share = u_flat.shape[0] // parts
        each = peers // parts
        copies = [pltpu.make_async_copy(res_hbm, res_ref, sems.at[parts])]
        for part in range(parts):
            at = pl.ds(part * share, share)
            copies.append(pltpu.make_async_copy(u_hbm.at[at], u_ref.at[at], sems.at[part]))
        for copy in copies:
            copy.start()
        copies[0].wait()
        half = res_ref[...].astype(BF16)
        for part in range(parts):
            copies[part + 1].wait()
            back = dot_nt(half, u_ref[part * share : (part + 1) * share, :])
            for k in range(each):
                out_ref[part * each + k] = back[:, k * wide : (k + 1) * wide].astype(BF16)

    def fill_left(in_ref, bound_ref, left_ref):
        for i in range(rows):
            piece = in_ref[i, :, 0:wide].astype(F32)
            stacked = jnp.concatenate([piece] * cols, axis=0)
            left_ref[:, i * wide : (i + 1) * wide] = jnp.where(
                kept_lanes(bound_ref, i), stacked, 0.0
            ).astype(BF16)

    def grad_kernel(in_ref, bound_ref, v_ref, out_ref, left_ref):
        fill_left(in_ref, bound_ref, left_ref)
        out_ref[...] = dot_nn(left_ref[...], v_ref[...])

    def grad_norm_kernel(in_ref, bound_ref, v_ref, out_ref, left_ref):
        fill_left(in_ref, bound_ref, left_ref)
        out_ref[0:tall, :] = dot_nn(left_ref[...], v_ref[...])
        norm = jnp.sum(gather_sum(in_ref, wide, 128), axis=1, keepdims=True)
        out_ref[tall : tall + dens, :] = jnp.broadcast_to(norm, (dens, patch))

    def coefficients(grad, bound_ref, v_ref, out_ref):
        half = grad.astype(BF16)
        for i in range(0, rows, 2):
            both = dot_nt(half, v_ref[i * wide : (i + 2) * wide, :])
            for k in range(2):
                part = jnp.where(
                    kept_lanes(bound_ref, i + k), both[:, k * wide : (k + 1) * wide], 0.0
                )
                total = part[0:dens]
                for j in range(1, cols):
                    total = total + part[j * dens : (j + 1) * dens]
                out_ref[i + k, :, 0:wide] = total.astype(BF16)

    def norm_of(grad):
        line = jnp.sum(grad * grad, axis=1, keepdims=True)
        total = line[0:dens]
        for j in range(1, line.shape[0] // dens):
            total = total + line[j * dens : (j + 1) * dens]
        return total

    def coef_kernel(p0_ref, p2_ref, p4_ref, p6_ref, bound_ref, v_ref, out_ref, grad_ref):
        grad = (p0_ref[...].astype(F32) + p2_ref[...].astype(F32)) + (
            p4_ref[...].astype(F32) + p6_ref[...].astype(F32)
        )
        grad_ref[...] = grad
        coefficients(grad, bound_ref, v_ref, out_ref)
        mine = spread(norm_of(grad))
        for i in range(rows):
            out_ref[i, :, wide : wide + 128] = mine

    def image_of(in_ref, u_ref):
        left = jnp.concatenate([in_ref[c, :, 0:wide] for c in range(peers)], axis=1)
        return dot_nn(left, u_ref[...])

    def image_back_kernel(in_ref, u_ref, image_ref, gsq_ref, out_ref):
        image = image_of(in_ref, u_ref)
        image_ref[...] = image
        gsq_ref[...] = jnp.broadcast_to(
            jnp.sum(gather_sum(in_ref, wide, 128), axis=1, keepdims=True), (dens, 128)
        )
        high = image.astype(BF16)
        low = (image - high.astype(F32)).astype(BF16)
        both = dot_nt(jnp.concatenate([high, low], axis=0), u_ref[...])
        back = both[0:dens] + both[dens : 2 * dens]
        mine = spread(norm_of(image))
        for peer in range(peers):
            out_ref[peer, :, 0:wide] = back[:, peer * wide : (peer + 1) * wide].astype(BF16)
            out_ref[peer, :, wide : wide + 128] = mine

    far_low = wide + 128

    def coef_far_kernel(
        p0_ref, p2_ref, p4_ref, p6_ref, grad_ref, gsq_ref, bound_ref, v_ref, far_ref,
        out_ref, first_ref, second_ref, step_ref, even_ref,
    ):
        wave = (p0_ref[...].astype(F32) + p2_ref[...].astype(F32)) + (
            p4_ref[...].astype(F32) + p6_ref[...].astype(F32)
        )
        isq = jnp.sum(wave[tall : tall + dens, 0:128], axis=1, keepdims=True)
        step = gsq_ref[:, 0:1] / (isq + 1e-6)
        step_ref[...] = jnp.broadcast_to(step, (dens, 128))
        steps = jnp.concatenate([step] * cols, axis=0)
        first = steps * grad_ref[...]
        second = grad_ref[...] - steps * wave[0:tall]
        first_ref[...] = first
        second_ref[...] = second
        coefficients(second, bound_ref, v_ref, out_ref)
        mine = spread(norm_of(second))
        lines = [
            jnp.concatenate([x[j * dens : (j + 1) * dens] for j in range(cols)], axis=1)
            for x in (first, second)
        ]
        left = jnp.concatenate(lines, axis=0).astype(BF16)
        even = dot_nt(left, far_ref[0])
        odd = dot_nt(left, far_ref[1])
        even_ref[...] = jnp.concatenate([even[0:dens], even[dens : 2 * dens]], axis=1).astype(BF16)
        send = jnp.concatenate([odd[0:dens], odd[dens : 2 * dens]], axis=1).astype(BF16)
        for i in range(rows):
            out_ref[i, :, wide : wide + 128] = mine
            out_ref[i, :, far_low : far_low + 2 * patch] = send

    def image_last_kernel(in_ref, u_ref, image_ref, gsq_ref, out_ref):
        image = image_of(in_ref, u_ref)
        image_ref[...] = image
        gsq_ref[...] = jnp.broadcast_to(
            jnp.sum(gather_sum(in_ref, wide, 128), axis=1, keepdims=True), (dens, 128)
        )
        here = lax.broadcasted_iota(jnp.int32, (dens, 128), 0) == lax.broadcasted_iota(
            jnp.int32, (dens, 128), 1
        )
        line = jnp.sum(jnp.where(here, norm_of(image), 0.0), axis=0, keepdims=True)
        for peer in range(devices):
            out_ref[peer] = line

    def route_kernel(target_ref, order_ref, even_ref, in_ref, keep_ref, give_ref):
        row, col = lax.axis_index("row"), lax.axis_index("col")
        for m in range(n_row):
            mine = order_ref[lax.bitwise_xor(row, m) * peers + col]
            total = jnp.zeros((dens, 2 * patch), F32)
            if m == n_row // 2:
                total = even_ref[...].astype(F32) * jnp.where(col % 2 == 0, 1.0, 0.0)
            for source in range(peers):
                hit = jnp.where(target_ref[row * blocks + 1, source] == mine, 1.0, 0.0)
                piece = in_ref[source, :, far_low : far_low + 2 * patch].astype(F32)
                total = total + piece * hit
            out_ref = keep_ref if m % 2 == 0 else give_ref
            out_ref[m // 2] = total.astype(BF16)

    def pair_kernel(own_ref, other_ref, out_ref):
        out_ref[0:tall, :] = (own_ref[0:tall] + other_ref[0:tall]).astype(BF16)
        low = slice(tall, tall + dens)
        out_ref[low, 0:128] = spread(own_ref[low, 0:1] + other_ref[low, 0:1])
        out_ref[low, 128:patch] = jnp.zeros((dens, patch - 128), BF16)

    def finish_kernel(
        norm_ref, gsq_ref, first_ref, second_ref, res_ref, image1_ref, image2_ref, step_ref,
        f0_ref, f2_ref, f4_ref, f6_ref, side_ref, dens_ref, out_res_ref, out_far_ref,
    ):
        line = norm_ref[0]
        for source in range(1, devices):
            line = line + norm_ref[source]
        here = lax.broadcasted_iota(jnp.int32, (dens, 128), 0) == lax.broadcasted_iota(
            jnp.int32, (dens, 128), 1
        )
        isq = jnp.sum(jnp.where(here, line, 0.0), axis=1, keepdims=True)
        step = gsq_ref[:, 0:1] / (isq + 1e-6)
        for j in range(cols):
            at = slice(j * dens, (j + 1) * dens)
            dens_ref[:, j * patch : (j + 1) * patch] = first_ref[at] + step * second_ref[at]
        out_res_ref[...] = (
            res_ref[...] - step_ref[:, 0:1] * image1_ref[...] - step * image2_ref[...]
        )
        both = side_ref[...].astype(F32) * jnp.where(lax.axis_index("col") % 2 == 0, 1.0, 0.0)
        for ref in (f0_ref, f2_ref, f4_ref, f6_ref):
            both = both + ref[...].astype(F32)
        field = both[:, 0:patch] + step * both[:, patch : 2 * patch]
        for d in range(dens):
            out_far_ref[:, d * patch : (d + 1) * patch] = field[d : d + 1]

    def row_shift(x, k):
        return lax.ppermute(x, "row", [(i, i ^ k) for i in range(n_row)])

    def over_rows(part):
        other = row_shift(part, 1)
        if part.shape[0] > tall:
            (half,) = call(pair_kernel, [(part.shape, BF16)], [part, other])
        else:
            half = (part + other).astype(BF16)
        half = lax.optimization_barrier(half)
        return [half] + [row_shift(half, k) for k in (2, 4, 6)]

    def over_col(x):
        return lax.all_to_all(x, "col", split_axis=0, concat_axis=0, tiled=True)

    left_scratch = (pltpu.VMEM((tall, rows * wide), BF16),)
    dma = pltpu.SemaphoreType.DMA
    sent, u_all = call(
        back_kernel,
        [((peers, dens, wide), BF16), (u_flat.shape, BF16)],
        [pltpu.with_memory_space_constraint(right_side, pltpu.HBM), u_flat],
        hbm=(0, 1),
        keep=(1,),
        scratch=(pltpu.VMEM((dens, patch), F32), dma((parts + 1,))),
    )
    sent, v_flat = lax.optimization_barrier((sent, v_factors.reshape(rows * wide, patch)))
    v_all = pltpu.with_memory_space_constraint(v_flat, pltpu.VMEM)
    landed, known = lax.optimization_barrier((over_col(sent), ranks))
    bound = jnp.repeat(known.T, dens, axis=0)
    (part,) = call(
        grad_kernel, [((tall, patch), F32)], [landed, bound, v_all], scratch=left_scratch
    )
    sent, grad = call(
        coef_kernel,
        [((rows, dens, wide + 128), BF16), ((tall, patch), F32)],
        over_rows(part) + [bound, v_all],
    )
    image1, gsq1, sent = call(
        image_back_kernel,
        [((dens, patch), F32), ((dens, 128), F32), ((peers, dens, wide + 128), BF16)],
        [over_col(sent), u_all],
    )
    (part,) = call(
        grad_norm_kernel,
        [((tall + dens, patch), F32)],
        [over_col(sent), bound, v_all],
        scratch=left_scratch,
    )
    sent, first, second, step1, even = call(
        coef_far_kernel,
        [
            ((rows, dens, far_low + 2 * patch), BF16),
            ((tall, patch), F32),
            ((tall, patch), F32),
            ((dens, 128), F32),
            ((dens, 2 * patch), BF16),
        ],
        over_rows(part) + [grad, gsq1, bound, v_all, far_all],
    )
    landed = over_col(sent)
    image2, gsq2, sent = call(
        image_last_kernel,
        [((dens, patch), F32), ((dens, 128), F32), ((devices, 1, 128), F32)],
        [landed, u_all],
    )
    norms = lax.all_to_all(sent, ("row", "col"), split_axis=0, concat_axis=0, tiled=True)
    even, landed, image2 = lax.optimization_barrier((even, landed, image2))
    keep, give = call(
        route_kernel,
        [((n_row // 2, dens, 2 * patch), BF16)] * 2,
        [block_target, recv_order, even, landed],
        smem=(0, 1),
    )
    near = keep + row_shift(give, 1)
    pieces = [near[0]] + [row_shift(near[k], 2 * k) for k in range(1, n_row // 2)]
    side = lax.ppermute(even, "col", [(c, c ^ 1) for c in range(peers)])
    densities, residual, far_field = call(
        finish_kernel,
        [((dens, cols * patch), F32), ((dens, patch), F32), ((1, dens * patch), F32)],
        [norms, gsq2, first, second, right_side, image1, image2, step1] + pieces + [side],
    )
    return densities, residual, far_field


def solution(mesh):
    return jax.shard_map(
        per_device,
        mesh=mesh,
        in_specs=(
            P(None, ("row", "col")),
            P(("row", "col"), None, None, None),
            P("row", "col", None, None),
            P("row", "col"),
            P("row", None, "col"),
            P(),
            P(),
        ),
        out_specs=(P(None, "col"), P(None, ("row", "col")), P(("row", "col"), None)),
        check_vma=False,
    )
```

```python
import jax
import jax.numpy as jnp
from jax import lax
from jax.experimental import pallas as pl
from jax.experimental.pallas import tpu as pltpu
from jax.sharding import PartitionSpec as P


F32, BF16 = jnp.float32, jnp.bfloat16
MIB = 1 << 20


def dot_nt(a, b):
    return lax.dot_general(a, b, (((1,), (1,)), ((), ())), preferred_element_type=F32)


def dot_nn(a, b):
    return lax.dot_general(a, b, (((1,), (0,)), ((), ())), preferred_element_type=F32)


def spread(value):
    high = value.astype(BF16).astype(F32)
    rest = value - high
    mid = rest.astype(BF16).astype(F32)
    low = rest - mid
    lane = lax.broadcasted_iota(jnp.int32, (value.shape[0], 128), 1)
    zero = jnp.zeros((value.shape[0], 128), F32)
    return jnp.where(
        lane == 0, high, jnp.where(lane == 1, mid, jnp.where(lane == 2, low, zero))
    ).astype(BF16)


def gather_sum(ref, low, width):
    total = ref[0, :, low : low + width].astype(F32)
    for source in range(1, ref.shape[0]):
        total = total + ref[source, :, low : low + width].astype(F32)
    return total


def call(kernel, outs, args, smem=(), hbm=(), keep=(), scratch=(), limit=8, smem_out=False):
    vm = pl.BlockSpec(memory_space=pltpu.VMEM)
    sm = pl.BlockSpec(memory_space=pltpu.SMEM)
    far_away = pl.BlockSpec(memory_space=pltpu.HBM)
    return pl.pallas_call(
        kernel,
        out_shape=tuple(
            pltpu.VMEM(s, d) if at in keep else jax.ShapeDtypeStruct(s, d)
            for at, (s, d) in enumerate(outs)
        ),
        in_specs=[
            sm if at in smem else far_away if at in hbm else vm for at in range(len(args))
        ],
        out_specs=tuple(sm if smem_out else vm for _ in outs),
        scratch_shapes=list(scratch),
        compiler_params=pltpu.CompilerParams(vmem_limit_bytes=limit * MIB),
    )(*args)


def per_device(right_side, u_factors, v_factors, ranks, far_blocks, block_target, recv_order):
    dens = right_side.shape[0]
    all_cols, slots, patch = u_factors.shape[1:]
    rows, cols = v_factors.shape[:2]
    peers = all_cols // cols
    wide = cols * slots
    n_row = lax.axis_size("row")
    devices = n_row * peers
    tall = cols * dens
    blocks = far_blocks.shape[0]

    u_flat = pltpu.with_memory_space_constraint(
        u_factors.reshape(all_cols * slots, patch), pltpu.HBM
    )
    far_all = pltpu.with_memory_space_constraint(far_blocks, pltpu.VMEM)
    parts = 4

    def kept_lanes(bound_ref, row_patch):
        lane = lax.broadcasted_iota(jnp.int32, (tall, wide), 1)
        first = lax.broadcasted_iota(jnp.int32, (tall, wide), 0) // dens * slots
        at = lane - first
        return (at >= 0) & (at < bound_ref[:, row_patch : row_patch + 1])

    def back_kernel(res_hbm, u_hbm, out_ref, u_ref, res_ref, sems):
        share = u_flat.shape[0] // parts
        each = peers // parts
        copies = [pltpu.make_async_copy(res_hbm, res_ref, sems.at[parts])]
        for part in range(parts):
            at = pl.ds(part * share, share)
            copies.append(pltpu.make_async_copy(u_hbm.at[at], u_ref.at[at], sems.at[part]))
        for copy in copies:
            copy.start()
        copies[0].wait()
        half = res_ref[...].astype(BF16)
        for part in range(parts):
            copies[part + 1].wait()
            back = dot_nt(half, u_ref[part * share : (part + 1) * share, :])
            for k in range(each):
                out_ref[part * each + k] = back[:, k * wide : (k + 1) * wide].astype(BF16)

    def fill_left(in_ref, bound_ref, left_ref):
        for i in range(rows):
            piece = in_ref[i, :, 0:wide].astype(F32)
            stacked = jnp.concatenate([piece] * cols, axis=0)
            left_ref[:, i * wide : (i + 1) * wide] = jnp.where(
                kept_lanes(bound_ref, i), stacked, 0.0
            ).astype(BF16)

    def grad_kernel(in_ref, bound_ref, v_ref, out_ref, left_ref):
        fill_left(in_ref, bound_ref, left_ref)
        out_ref[...] = dot_nn(left_ref[...], v_ref[...])

    def grad_norm_kernel(in_ref, bound_ref, v_ref, out_ref, left_ref):
        fill_left(in_ref, bound_ref, left_ref)
        out_ref[0:tall, :] = dot_nn(left_ref[...], v_ref[...])
        norm = jnp.sum(gather_sum(in_ref, wide, 128), axis=1, keepdims=True)
        out_ref[tall : tall + dens, :] = jnp.broadcast_to(norm, (dens, patch))

    def coefficients(grad, bound_ref, v_ref, out_ref):
        half = grad.astype(BF16)
        for i in range(0, rows, 2):
            both = dot_nt(half, v_ref[i * wide : (i + 2) * wide, :])
            for k in range(2):
                part = jnp.where(
                    kept_lanes(bound_ref, i + k), both[:, k * wide : (k + 1) * wide], 0.0
                )
                total = part[0:dens]
                for j in range(1, cols):
                    total = total + part[j * dens : (j + 1) * dens]
                out_ref[i + k, :, 0:wide] = total.astype(BF16)

    def norm_of(grad):
        line = jnp.sum(grad * grad, axis=1, keepdims=True)
        total = line[0:dens]
        for j in range(1, line.shape[0] // dens):
            total = total + line[j * dens : (j + 1) * dens]
        return total

    def coef_kernel(p0_ref, p2_ref, p4_ref, p6_ref, bound_ref, v_ref, out_ref, grad_ref):
        grad = (p0_ref[...].astype(F32) + p2_ref[...].astype(F32)) + (
            p4_ref[...].astype(F32) + p6_ref[...].astype(F32)
        )
        grad_ref[...] = grad
        coefficients(grad, bound_ref, v_ref, out_ref)
        mine = spread(norm_of(grad))
        for i in range(rows):
            out_ref[i, :, wide : wide + 128] = mine

    def image_of(in_ref, u_ref):
        left = jnp.concatenate([in_ref[c, :, 0:wide] for c in range(peers)], axis=1)
        return dot_nn(left, u_ref[...])

    def image_back_kernel(in_ref, u_ref, image_ref, gsq_ref, out_ref):
        image = image_of(in_ref, u_ref)
        image_ref[...] = image
        gsq_ref[...] = jnp.broadcast_to(
            jnp.sum(gather_sum(in_ref, wide, 128), axis=1, keepdims=True), (dens, 128)
        )
        high = image.astype(BF16)
        low = (image - high.astype(F32)).astype(BF16)
        both = dot_nt(jnp.concatenate([high, low], axis=0), u_ref[...])
        back = both[0:dens] + both[dens : 2 * dens]
        mine = spread(norm_of(image))
        for peer in range(peers):
            out_ref[peer, :, 0:wide] = back[:, peer * wide : (peer + 1) * wide].astype(BF16)
            out_ref[peer, :, wide : wide + 128] = mine

    far_low = wide + 128

    def coef_far_kernel(
        p0_ref, p2_ref, p4_ref, p6_ref, grad_ref, gsq_ref, bound_ref, v_ref, far_ref,
        out_ref, first_ref, second_ref, step_ref, even_ref,
    ):
        wave = (p0_ref[...].astype(F32) + p2_ref[...].astype(F32)) + (
            p4_ref[...].astype(F32) + p6_ref[...].astype(F32)
        )
        isq = jnp.sum(wave[tall : tall + dens, 0:128], axis=1, keepdims=True)
        step = gsq_ref[:, 0:1] / (isq + 1e-6)
        step_ref[...] = jnp.broadcast_to(step, (dens, 128))
        steps = jnp.concatenate([step] * cols, axis=0)
        first = steps * grad_ref[...]
        second = grad_ref[...] - steps * wave[0:tall]
        first_ref[...] = first
        second_ref[...] = second
        coefficients(second, bound_ref, v_ref, out_ref)
        mine = spread(norm_of(second))
        lines = [
            jnp.concatenate([x[j * dens : (j + 1) * dens] for j in range(cols)], axis=1)
            for x in (first, second)
        ]
        left = jnp.concatenate(lines, axis=0).astype(BF16)
        even = dot_nt(left, far_ref[0])
        odd = dot_nt(left, far_ref[1])
        even_ref[...] = jnp.concatenate([even[0:dens], even[dens : 2 * dens]], axis=1).astype(BF16)
        send = jnp.concatenate([odd[0:dens], odd[dens : 2 * dens]], axis=1).astype(BF16)
        for i in range(rows):
            out_ref[i, :, wide : wide + 128] = mine
            out_ref[i, :, far_low : far_low + 2 * patch] = send

    def image_last_kernel(in_ref, u_ref, image_ref, gsq_ref, out_ref):
        image = image_of(in_ref, u_ref)
        image_ref[...] = image
        gsq_ref[...] = jnp.broadcast_to(
            jnp.sum(gather_sum(in_ref, wide, 128), axis=1, keepdims=True), (dens, 128)
        )
        here = lax.broadcasted_iota(jnp.int32, (dens, 128), 0) == lax.broadcasted_iota(
            jnp.int32, (dens, 128), 1
        )
        line = jnp.sum(jnp.where(here, norm_of(image), 0.0), axis=0, keepdims=True)
        for peer in range(devices):
            out_ref[peer] = line

    def slot_kernel(target_ref, order_ref, slot_ref):
        row, col = lax.axis_index("row"), lax.axis_index("col")
        mine = [order_ref[lax.bitwise_xor(row, m) * peers + col] for m in range(n_row)]
        for source in range(peers):
            target = target_ref[row * blocks + 1, source]
            slot = jnp.int32(n_row)
            for m in range(n_row):
                slot = jnp.where(target == mine[m], m, slot)
            slot_ref[source] = slot

    def route_kernel(slot_ref, even_ref, in_ref, keep_ref, give_ref, sum_ref):
        sum_ref[...] = jnp.zeros_like(sum_ref)
        sum_ref[n_row // 2] = even_ref[...].astype(F32) * jnp.where(
            lax.axis_index("col") % 2 == 0, 1.0, 0.0
        )
        for source in range(peers):
            slot = slot_ref[source]

            @pl.when(slot < n_row)
            def _():
                piece = in_ref[source, :, far_low : far_low + 2 * patch].astype(F32)
                sum_ref[slot] = sum_ref[slot] + piece

        for m in range(n_row):
            out_ref = keep_ref if m % 2 == 0 else give_ref
            out_ref[m // 2] = sum_ref[m].astype(BF16)

    def pair_kernel(own_ref, other_ref, out_ref):
        out_ref[0:tall, :] = (own_ref[0:tall] + other_ref[0:tall]).astype(BF16)
        low = slice(tall, tall + dens)
        out_ref[low, 0:128] = spread(own_ref[low, 0:1] + other_ref[low, 0:1])
        out_ref[low, 128:patch] = jnp.zeros((dens, patch - 128), BF16)

    def finish_kernel(
        norm_ref, gsq_ref, first_ref, second_ref, res_ref, image1_ref, image2_ref, step_ref,
        f0_ref, f2_ref, f4_ref, f6_ref, side_ref, dens_ref, out_res_ref, out_far_ref,
    ):
        line = norm_ref[0]
        for source in range(1, devices):
            line = line + norm_ref[source]
        here = lax.broadcasted_iota(jnp.int32, (dens, 128), 0) == lax.broadcasted_iota(
            jnp.int32, (dens, 128), 1
        )
        isq = jnp.sum(jnp.where(here, line, 0.0), axis=1, keepdims=True)
        step = gsq_ref[:, 0:1] / (isq + 1e-6)
        for j in range(cols):
            at = slice(j * dens, (j + 1) * dens)
            dens_ref[:, j * patch : (j + 1) * patch] = first_ref[at] + step * second_ref[at]
        out_res_ref[...] = (
            res_ref[...] - step_ref[:, 0:1] * image1_ref[...] - step * image2_ref[...]
        )
        both = side_ref[...].astype(F32) * jnp.where(lax.axis_index("col") % 2 == 0, 1.0, 0.0)
        for ref in (f0_ref, f2_ref, f4_ref, f6_ref):
            both = both + ref[...].astype(F32)
        field = both[:, 0:patch] + step * both[:, patch : 2 * patch]
        for d in range(dens):
            out_far_ref[:, d * patch : (d + 1) * patch] = field[d : d + 1]

    def row_shift(x, k):
        return lax.ppermute(x, "row", [(i, i ^ k) for i in range(n_row)])

    def hops(halves):
        arrived = []
        for k, half in zip((2, 4, 6), halves):
            arrived.append(row_shift(half, k))
        return arrived

    def over_rows(part):
        other = row_shift(part, 1)
        if part.shape[0] > tall:
            (half,) = call(pair_kernel, [(part.shape, BF16)], [part, other])
        else:
            half = (part + other).astype(BF16)
        half = lax.optimization_barrier(half)
        return [half] + hops([half] * 3)

    def over_col(x):
        return lax.all_to_all(x, "col", split_axis=0, concat_axis=0, tiled=True)

    left_scratch = (pltpu.VMEM((tall, rows * wide), BF16),)
    dma = pltpu.SemaphoreType.DMA
    sent, u_all = call(
        back_kernel,
        [((peers, dens, wide), BF16), (u_flat.shape, BF16)],
        [pltpu.with_memory_space_constraint(right_side, pltpu.HBM), u_flat],
        hbm=(0, 1),
        keep=(1,),
        scratch=(pltpu.VMEM((dens, patch), F32), dma((parts + 1,))),
    )
    sent, v_flat = lax.optimization_barrier((sent, v_factors.reshape(rows * wide, patch)))
    v_all = pltpu.with_memory_space_constraint(v_flat, pltpu.VMEM)
    landed, known = lax.optimization_barrier((over_col(sent), ranks))
    bound = jnp.repeat(known.T, dens, axis=0)
    (part,) = call(
        grad_kernel, [((tall, patch), F32)], [landed, bound, v_all], scratch=left_scratch
    )
    part, *tables = lax.optimization_barrier((part, block_target, recv_order))
    (slot,) = call(slot_kernel, [((peers,), jnp.int32)], tables, smem=(0, 1), smem_out=True)
    *arrived, slot = lax.optimization_barrier((*over_rows(part), slot))
    sent, grad = call(
        coef_kernel,
        [((rows, dens, wide + 128), BF16), ((tall, patch), F32)],
        arrived + [bound, v_all],
    )
    image1, gsq1, sent = call(
        image_back_kernel,
        [((dens, patch), F32), ((dens, 128), F32), ((peers, dens, wide + 128), BF16)],
        [over_col(sent), u_all],
    )
    (part,) = call(
        grad_norm_kernel,
        [((tall + dens, patch), F32)],
        [over_col(sent), bound, v_all],
        scratch=left_scratch,
    )
    sent, first, second, step1, even = call(
        coef_far_kernel,
        [
            ((rows, dens, far_low + 2 * patch), BF16),
            ((tall, patch), F32),
            ((tall, patch), F32),
            ((dens, 128), F32),
            ((dens, 2 * patch), BF16),
        ],
        over_rows(part) + [grad, gsq1, bound, v_all, far_all],
    )
    landed = over_col(sent)
    image2, gsq2, sent = call(
        image_last_kernel,
        [((dens, patch), F32), ((dens, 128), F32), ((devices, 1, 128), F32)],
        [landed, u_all],
    )
    norms = lax.all_to_all(sent, ("row", "col"), split_axis=0, concat_axis=0, tiled=True)
    even, landed, image2 = lax.optimization_barrier((even, landed, image2))
    keep, give = call(
        route_kernel,
        [((n_row // 2, dens, 2 * patch), BF16)] * 2,
        [slot, even, landed],
        smem=(0,),
        scratch=(pltpu.VMEM((n_row, dens, 2 * patch), F32),),
    )
    near = keep + row_shift(give, 1)
    pieces = [near[0]] + hops([near[k] for k in range(1, n_row // 2)])
    side = lax.ppermute(even, "col", [(c, c ^ 1) for c in range(peers)])
    densities, residual, far_field = call(
        finish_kernel,
        [((dens, cols * patch), F32), ((dens, patch), F32), ((1, dens * patch), F32)],
        [norms, gsq2, first, second, right_side, image1, image2, step1] + pieces + [side],
    )
    return densities, residual, far_field


def solution(mesh):
    return jax.shard_map(
        per_device,
        mesh=mesh,
        in_specs=(
            P(None, ("row", "col")),
            P(("row", "col"), None, None, None),
            P("row", "col", None, None),
            P("row", "col"),
            P("row", None, "col"),
            P(),
            P(),
        ),
        out_specs=(P(None, "col"), P(None, ("row", "col")), P(("row", "col"), None)),
        check_vma=False,
    )
```

```python
import jax
import jax.numpy as jnp
from jax import lax
from jax.experimental import pallas as pl
from jax.experimental.pallas import tpu as pltpu
from jax.sharding import PartitionSpec as P


F32, BF16 = jnp.float32, jnp.bfloat16
MIB = 1 << 20


def dot_nt(a, b):
    return lax.dot_general(a, b, (((1,), (1,)), ((), ())), preferred_element_type=F32)


def dot_nn(a, b):
    return lax.dot_general(a, b, (((1,), (0,)), ((), ())), preferred_element_type=F32)


def spread(value):
    high = value.astype(BF16).astype(F32)
    rest = value - high
    mid = rest.astype(BF16).astype(F32)
    low = rest - mid
    lane = lax.broadcasted_iota(jnp.int32, (value.shape[0], 128), 1)
    zero = jnp.zeros((value.shape[0], 128), F32)
    return jnp.where(
        lane == 0, high, jnp.where(lane == 1, mid, jnp.where(lane == 2, low, zero))
    ).astype(BF16)


def gather_sum(ref, low, width):
    total = ref[0, :, low : low + width].astype(F32)
    for source in range(1, ref.shape[0]):
        total = total + ref[source, :, low : low + width].astype(F32)
    return total


def call(kernel, outs, args, smem=(), hbm=(), keep=(), scratch=(), limit=8, smem_out=False):
    vm = pl.BlockSpec(memory_space=pltpu.VMEM)
    sm = pl.BlockSpec(memory_space=pltpu.SMEM)
    far_away = pl.BlockSpec(memory_space=pltpu.HBM)
    return pl.pallas_call(
        kernel,
        out_shape=tuple(
            pltpu.VMEM(s, d) if at in keep else jax.ShapeDtypeStruct(s, d)
            for at, (s, d) in enumerate(outs)
        ),
        in_specs=[
            sm if at in smem else far_away if at in hbm else vm for at in range(len(args))
        ],
        out_specs=tuple(sm if smem_out else vm for _ in outs),
        scratch_shapes=list(scratch),
        compiler_params=pltpu.CompilerParams(vmem_limit_bytes=limit * MIB),
    )(*args)


def per_device(right_side, u_factors, v_factors, ranks, far_blocks, block_target, recv_order):
    dens = right_side.shape[0]
    all_cols, slots, patch = u_factors.shape[1:]
    rows, cols = v_factors.shape[:2]
    peers = all_cols // cols
    wide = cols * slots
    n_row = lax.axis_size("row")
    devices = n_row * peers
    tall = cols * dens
    blocks = far_blocks.shape[0]

    u_flat = pltpu.with_memory_space_constraint(
        u_factors.reshape(all_cols * slots, patch), pltpu.HBM
    )
    far_all = pltpu.with_memory_space_constraint(far_blocks, pltpu.VMEM)
    parts = 4

    def kept_lanes(bound_ref, row_patch):
        lane = lax.broadcasted_iota(jnp.int32, (tall, wide), 1)
        first = lax.broadcasted_iota(jnp.int32, (tall, wide), 0) // dens * slots
        at = lane - first
        return (at >= 0) & (at < bound_ref[:, row_patch : row_patch + 1])

    def back_kernel(res_hbm, u_hbm, out_ref, u_ref, res_ref, sems):
        share = u_flat.shape[0] // parts
        each = peers // parts
        copies = [pltpu.make_async_copy(res_hbm, res_ref, sems.at[parts])]
        for part in range(parts):
            at = pl.ds(part * share, share)
            copies.append(pltpu.make_async_copy(u_hbm.at[at], u_ref.at[at], sems.at[part]))
        for copy in copies:
            copy.start()
        copies[0].wait()
        half = res_ref[...].astype(BF16)
        for part in range(parts):
            copies[part + 1].wait()
            back = dot_nt(half, u_ref[part * share : (part + 1) * share, :])
            for k in range(each):
                out_ref[part * each + k] = back[:, k * wide : (k + 1) * wide].astype(BF16)

    def fill_left(in_ref, bound_ref, left_ref):
        for i in range(rows):
            piece = in_ref[i, :, 0:wide].astype(F32)
            stacked = jnp.concatenate([piece] * cols, axis=0)
            left_ref[:, i * wide : (i + 1) * wide] = jnp.where(
                kept_lanes(bound_ref, i), stacked, 0.0
            ).astype(BF16)

    def grad_kernel(in_ref, bound_ref, v_ref, out_ref, left_ref):
        fill_left(in_ref, bound_ref, left_ref)
        out_ref[...] = dot_nn(left_ref[...], v_ref[...])

    def grad_norm_kernel(in_ref, bound_ref, v_ref, out_ref, left_ref):
        fill_left(in_ref, bound_ref, left_ref)
        out_ref[0:tall, :] = dot_nn(left_ref[...], v_ref[...])
        norm = jnp.sum(gather_sum(in_ref, wide, 128), axis=1, keepdims=True)
        out_ref[tall : tall + dens, :] = jnp.broadcast_to(norm, (dens, patch))

    def flip_kernel(in_ref, out_ref):
        for at in range(0, in_ref.shape[0], patch):
            out_ref[:, at : at + patch] = in_ref[at : at + patch, :].T

    def flip_far_kernel(in_ref, out_ref):
        for block in range(blocks):
            for at in range(0, in_ref.shape[2], patch):
                out_ref[block, at : at + patch, :] = in_ref[block, :, at : at + patch].T

    def flip(kernel, x, shape):
        (out,) = call(kernel, [(shape, BF16)], [x], keep=(0,))
        return out

    def coefficients(grad, bound_ref, v_ref, out_ref):
        half = grad.astype(BF16)
        for i in range(0, rows, 2):
            both = dot_nn(half, v_ref[:, i * wide : (i + 2) * wide])
            for k in range(2):
                part = jnp.where(
                    kept_lanes(bound_ref, i + k), both[:, k * wide : (k + 1) * wide], 0.0
                )
                total = part[0:dens]
                for j in range(1, cols):
                    total = total + part[j * dens : (j + 1) * dens]
                out_ref[i + k, :, 0:wide] = total.astype(BF16)

    def norm_of(grad):
        line = jnp.sum(grad * grad, axis=1, keepdims=True)
        total = line[0:dens]
        for j in range(1, line.shape[0] // dens):
            total = total + line[j * dens : (j + 1) * dens]
        return total

    def coef_kernel(p0_ref, p2_ref, p4_ref, p6_ref, bound_ref, v_ref, out_ref, grad_ref):
        grad = (p0_ref[...].astype(F32) + p2_ref[...].astype(F32)) + (
            p4_ref[...].astype(F32) + p6_ref[...].astype(F32)
        )
        grad_ref[...] = grad
        coefficients(grad, bound_ref, v_ref, out_ref)
        mine = spread(norm_of(grad))
        for i in range(rows):
            out_ref[i, :, wide : wide + 128] = mine

    def image_of(in_ref, u_ref):
        left = jnp.concatenate([in_ref[c, :, 0:wide] for c in range(peers)], axis=1)
        return dot_nn(left, u_ref[...])

    def image_back_kernel(in_ref, u_ref, ut_ref, image_ref, gsq_ref, out_ref):
        image = image_of(in_ref, u_ref)
        image_ref[...] = image
        gsq_ref[...] = jnp.broadcast_to(
            jnp.sum(gather_sum(in_ref, wide, 128), axis=1, keepdims=True), (dens, 128)
        )
        high = image.astype(BF16)
        low = (image - high.astype(F32)).astype(BF16)
        both = dot_nn(jnp.concatenate([high, low], axis=0), ut_ref[...])
        back = both[0:dens] + both[dens : 2 * dens]
        mine = spread(norm_of(image))
        for peer in range(peers):
            out_ref[peer, :, 0:wide] = back[:, peer * wide : (peer + 1) * wide].astype(BF16)
            out_ref[peer, :, wide : wide + 128] = mine

    far_low = wide + 128

    def coef_far_kernel(
        p0_ref, p2_ref, p4_ref, p6_ref, grad_ref, gsq_ref, bound_ref, v_ref, far_ref,
        out_ref, first_ref, second_ref, step_ref, even_ref,
    ):
        wave = (p0_ref[...].astype(F32) + p2_ref[...].astype(F32)) + (
            p4_ref[...].astype(F32) + p6_ref[...].astype(F32)
        )
        isq = jnp.sum(wave[tall : tall + dens, 0:128], axis=1, keepdims=True)
        step = gsq_ref[:, 0:1] / (isq + 1e-6)
        step_ref[...] = jnp.broadcast_to(step, (dens, 128))
        steps = jnp.concatenate([step] * cols, axis=0)
        first = steps * grad_ref[...]
        second = grad_ref[...] - steps * wave[0:tall]
        first_ref[...] = first
        second_ref[...] = second
        coefficients(second, bound_ref, v_ref, out_ref)
        mine = spread(norm_of(second))
        lines = [
            jnp.concatenate([x[j * dens : (j + 1) * dens] for j in range(cols)], axis=1)
            for x in (first, second)
        ]
        left = jnp.concatenate(lines, axis=0).astype(BF16)
        even = dot_nn(left, far_ref[0])
        odd = dot_nn(left, far_ref[1])
        even_ref[...] = jnp.concatenate([even[0:dens], even[dens : 2 * dens]], axis=1).astype(BF16)
        send = jnp.concatenate([odd[0:dens], odd[dens : 2 * dens]], axis=1).astype(BF16)
        for i in range(rows):
            out_ref[i, :, wide : wide + 128] = mine
            out_ref[i, :, far_low : far_low + 2 * patch] = send

    def image_last_kernel(in_ref, u_ref, image_ref, gsq_ref, out_ref):
        image = image_of(in_ref, u_ref)
        image_ref[...] = image
        gsq_ref[...] = jnp.broadcast_to(
            jnp.sum(gather_sum(in_ref, wide, 128), axis=1, keepdims=True), (dens, 128)
        )
        here = lax.broadcasted_iota(jnp.int32, (dens, 128), 0) == lax.broadcasted_iota(
            jnp.int32, (dens, 128), 1
        )
        line = jnp.sum(jnp.where(here, norm_of(image), 0.0), axis=0, keepdims=True)
        for peer in range(devices):
            out_ref[peer] = line

    def slot_kernel(target_ref, order_ref, slot_ref):
        row, col = lax.axis_index("row"), lax.axis_index("col")
        mine = [order_ref[lax.bitwise_xor(row, m) * peers + col] for m in range(n_row)]
        for source in range(peers):
            target = target_ref[row * blocks + 1, source]
            slot = jnp.int32(n_row)
            for m in range(n_row):
                slot = jnp.where(target == mine[m], m, slot)
            slot_ref[source] = slot

    def route_kernel(slot_ref, even_ref, in_ref, keep_ref, give_ref, sum_ref):
        sum_ref[...] = jnp.zeros_like(sum_ref)
        sum_ref[n_row // 2] = even_ref[...].astype(F32) * jnp.where(
            lax.axis_index("col") % 2 == 0, 1.0, 0.0
        )
        for source in range(peers):
            slot = slot_ref[source]

            @pl.when(slot < n_row)
            def _():
                piece = in_ref[source, :, far_low : far_low + 2 * patch].astype(F32)
                sum_ref[slot] = sum_ref[slot] + piece

        for m in range(n_row):
            out_ref = keep_ref if m % 2 == 0 else give_ref
            out_ref[m // 2] = sum_ref[m].astype(BF16)

    def pair_kernel(own_ref, other_ref, out_ref):
        out_ref[0:tall, :] = (own_ref[0:tall] + other_ref[0:tall]).astype(BF16)
        low = slice(tall, tall + dens)
        out_ref[low, 0:128] = spread(own_ref[low, 0:1] + other_ref[low, 0:1])
        out_ref[low, 128:patch] = jnp.zeros((dens, patch - 128), BF16)

    def finish_kernel(
        norm_ref, gsq_ref, first_ref, second_ref, res_ref, image1_ref, image2_ref, step_ref,
        f0_ref, f2_ref, f4_ref, f6_ref, side_ref, dens_ref, out_res_ref, out_far_ref,
    ):
        line = norm_ref[0]
        for source in range(1, devices):
            line = line + norm_ref[source]
        here = lax.broadcasted_iota(jnp.int32, (dens, 128), 0) == lax.broadcasted_iota(
            jnp.int32, (dens, 128), 1
        )
        isq = jnp.sum(jnp.where(here, line, 0.0), axis=1, keepdims=True)
        step = gsq_ref[:, 0:1] / (isq + 1e-6)
        for j in range(cols):
            at = slice(j * dens, (j + 1) * dens)
            dens_ref[:, j * patch : (j + 1) * patch] = first_ref[at] + step * second_ref[at]
        out_res_ref[...] = (
            res_ref[...] - step_ref[:, 0:1] * image1_ref[...] - step * image2_ref[...]
        )
        both = side_ref[...].astype(F32) * jnp.where(lax.axis_index("col") % 2 == 0, 1.0, 0.0)
        for ref in (f0_ref, f2_ref, f4_ref, f6_ref):
            both = both + ref[...].astype(F32)
        field = both[:, 0:patch] + step * both[:, patch : 2 * patch]
        for d in range(dens):
            out_far_ref[:, d * patch : (d + 1) * patch] = field[d : d + 1]

    def row_shift(x, k):
        return lax.ppermute(x, "row", [(i, i ^ k) for i in range(n_row)])

    def hops(halves):
        arrived = []
        for k, half in zip((2, 4, 6), halves):
            arrived.append(row_shift(half, k))
        return arrived

    def over_rows(part):
        other = row_shift(part, 1)
        if part.shape[0] > tall:
            (half,) = call(pair_kernel, [(part.shape, BF16)], [part, other])
        else:
            half = (part + other).astype(BF16)
        half = lax.optimization_barrier(half)
        return [half] + hops([half] * 3)

    def over_col(x):
        return lax.all_to_all(x, "col", split_axis=0, concat_axis=0, tiled=True)

    left_scratch = (pltpu.VMEM((tall, rows * wide), BF16),)
    dma = pltpu.SemaphoreType.DMA
    sent, u_all = call(
        back_kernel,
        [((peers, dens, wide), BF16), (u_flat.shape, BF16)],
        [pltpu.with_memory_space_constraint(right_side, pltpu.HBM), u_flat],
        hbm=(0, 1),
        keep=(1,),
        scratch=(pltpu.VMEM((dens, patch), F32), dma((parts + 1,))),
    )
    sent, v_flat = lax.optimization_barrier((sent, v_factors.reshape(rows * wide, patch)))
    v_all = pltpu.with_memory_space_constraint(v_flat, pltpu.VMEM)
    landed, known = lax.optimization_barrier((over_col(sent), ranks))
    bound = jnp.repeat(known.T, dens, axis=0)
    (part,) = call(
        grad_kernel, [((tall, patch), F32)], [landed, bound, v_all], scratch=left_scratch
    )
    part, v_now, u_now = lax.optimization_barrier((part, v_all, u_all))
    v_flip = flip(flip_kernel, v_now, (patch, v_now.shape[0]))
    u_flip = flip(flip_kernel, u_now, (patch, u_now.shape[0]))
    *arrived, v_flip, u_flip = lax.optimization_barrier((*over_rows(part), v_flip, u_flip))
    sent, grad = call(
        coef_kernel,
        [((rows, dens, wide + 128), BF16), ((tall, patch), F32)],
        arrived + [bound, v_flip],
    )
    image1, gsq1, sent = call(
        image_back_kernel,
        [((dens, patch), F32), ((dens, 128), F32), ((peers, dens, wide + 128), BF16)],
        [over_col(sent), u_all, u_flip],
    )
    (part,) = call(
        grad_norm_kernel,
        [((tall + dens, patch), F32)],
        [over_col(sent), bound, v_all],
        scratch=left_scratch,
    )
    part, far_now, *tables = lax.optimization_barrier((part, far_all, block_target, recv_order))
    far_flip = flip(flip_far_kernel, far_now, (blocks, far_now.shape[2], patch))
    (slot,) = call(slot_kernel, [((peers,), jnp.int32)], tables, smem=(0, 1), smem_out=True)
    *arrived, far_flip, slot = lax.optimization_barrier((*over_rows(part), far_flip, slot))
    sent, first, second, step1, even = call(
        coef_far_kernel,
        [
            ((rows, dens, far_low + 2 * patch), BF16),
            ((tall, patch), F32),
            ((tall, patch), F32),
            ((dens, 128), F32),
            ((dens, 2 * patch), BF16),
        ],
        arrived + [grad, gsq1, bound, v_flip, far_flip],
    )
    landed = over_col(sent)
    image2, gsq2, sent = call(
        image_last_kernel,
        [((dens, patch), F32), ((dens, 128), F32), ((devices, 1, 128), F32)],
        [landed, u_all],
    )
    norms = lax.all_to_all(sent, ("row", "col"), split_axis=0, concat_axis=0, tiled=True)
    even, landed, image2 = lax.optimization_barrier((even, landed, image2))
    keep, give = call(
        route_kernel,
        [((n_row // 2, dens, 2 * patch), BF16)] * 2,
        [slot, even, landed],
        smem=(0,),
        scratch=(pltpu.VMEM((n_row, dens, 2 * patch), F32),),
    )
    near = keep + row_shift(give, 1)
    pieces = [near[0]] + hops([near[k] for k in range(1, n_row // 2)])
    side = lax.ppermute(even, "col", [(c, c ^ 1) for c in range(peers)])
    densities, residual, far_field = call(
        finish_kernel,
        [((dens, cols * patch), F32), ((dens, patch), F32), ((1, dens * patch), F32)],
        [norms, gsq2, first, second, right_side, image1, image2, step1] + pieces + [side],
    )
    return densities, residual, far_field


def solution(mesh):
    return jax.shard_map(
        per_device,
        mesh=mesh,
        in_specs=(
            P(None, ("row", "col")),
            P(("row", "col"), None, None, None),
            P("row", "col", None, None),
            P("row", "col"),
            P("row", None, "col"),
            P(),
            P(),
        ),
        out_specs=(P(None, "col"), P(None, ("row", "col")), P(("row", "col"), None)),
        check_vma=False,
    )
```

```python
import jax
import jax.numpy as jnp
from jax import lax
from jax.experimental import pallas as pl
from jax.experimental.pallas import tpu as pltpu
from jax.sharding import PartitionSpec as P


F32, BF16 = jnp.float32, jnp.bfloat16
MIB = 1 << 20


def dot_nn(a, b):
    return lax.dot_general(a, b, (((1,), (0,)), ((), ())), preferred_element_type=F32)


def spread(value):
    high = value.astype(BF16).astype(F32)
    rest = value - high
    mid = rest.astype(BF16).astype(F32)
    low = rest - mid
    lane = lax.broadcasted_iota(jnp.int32, (value.shape[0], 128), 1)
    zero = jnp.zeros((value.shape[0], 128), F32)
    return jnp.where(
        lane == 0, high, jnp.where(lane == 1, mid, jnp.where(lane == 2, low, zero))
    ).astype(BF16)


def gather_sum(ref, low, width):
    total = ref[0, :, low : low + width].astype(F32)
    for source in range(1, ref.shape[0]):
        total = total + ref[source, :, low : low + width].astype(F32)
    return total


def call(kernel, outs, args, smem=(), hbm=(), keep=(), scratch=(), limit=8, smem_out=False):
    vm = pl.BlockSpec(memory_space=pltpu.VMEM)
    sm = pl.BlockSpec(memory_space=pltpu.SMEM)
    far_away = pl.BlockSpec(memory_space=pltpu.HBM)
    return pl.pallas_call(
        kernel,
        out_shape=tuple(
            pltpu.VMEM(s, d) if at in keep else jax.ShapeDtypeStruct(s, d)
            for at, (s, d) in enumerate(outs)
        ),
        in_specs=[
            sm if at in smem else far_away if at in hbm else vm for at in range(len(args))
        ],
        out_specs=tuple(sm if smem_out else vm for _ in outs),
        scratch_shapes=list(scratch),
        compiler_params=pltpu.CompilerParams(vmem_limit_bytes=limit * MIB),
    )(*args)


def per_device(right_side, u_factors, v_factors, ranks, far_blocks, block_target, recv_order):
    dens = right_side.shape[0]
    all_cols, slots, patch = u_factors.shape[1:]
    rows, cols = v_factors.shape[:2]
    peers = all_cols // cols
    wide = cols * slots
    n_row = lax.axis_size("row")
    devices = n_row * peers
    tall = cols * dens
    blocks = far_blocks.shape[0]

    u_flat = pltpu.with_memory_space_constraint(
        u_factors.reshape(all_cols * slots, patch), pltpu.HBM
    )
    far_all = pltpu.with_memory_space_constraint(far_blocks, pltpu.VMEM)
    parts = 4

    def kept_lanes(bound_ref, row_patch):
        lane = lax.broadcasted_iota(jnp.int32, (tall, wide), 1)
        first = lax.broadcasted_iota(jnp.int32, (tall, wide), 0) // dens * slots
        at = lane - first
        return (at >= 0) & (at < bound_ref[:, row_patch : row_patch + 1])

    def back_kernel(res_hbm, u_hbm, out_ref, u_ref, ut_ref, res_ref, sems):
        share = u_flat.shape[0] // parts
        each = peers // parts
        copies = [pltpu.make_async_copy(res_hbm, res_ref, sems.at[parts])]
        for part in range(parts):
            at = pl.ds(part * share, share)
            copies.append(pltpu.make_async_copy(u_hbm.at[at], u_ref.at[at], sems.at[part]))
        for copy in copies:
            copy.start()
        copies[0].wait()
        half = res_ref[...].astype(BF16)
        for part in range(parts):
            copies[part + 1].wait()
            turned = u_ref[part * share : (part + 1) * share, :].T
            ut_ref[:, part * share : (part + 1) * share] = turned
            back = dot_nn(half, turned)
            for k in range(each):
                out_ref[part * each + k] = back[:, k * wide : (k + 1) * wide].astype(BF16)

    def fill_left(in_ref, bound_ref, left_ref):
        for i in range(rows):
            piece = in_ref[i, :, 0:wide].astype(F32)
            stacked = jnp.concatenate([piece] * cols, axis=0)
            left_ref[:, i * wide : (i + 1) * wide] = jnp.where(
                kept_lanes(bound_ref, i), stacked, 0.0
            ).astype(BF16)

    def grad_kernel(in_ref, bound_ref, v_ref, out_ref, left_ref):
        fill_left(in_ref, bound_ref, left_ref)
        out_ref[...] = dot_nn(left_ref[...], v_ref[...])

    def grad_norm_kernel(in_ref, bound_ref, v_ref, out_ref, left_ref):
        fill_left(in_ref, bound_ref, left_ref)
        out_ref[0:tall, :] = dot_nn(left_ref[...], v_ref[...])
        norm = jnp.sum(gather_sum(in_ref, wide, 128), axis=1, keepdims=True)
        out_ref[tall : tall + dens, :] = jnp.broadcast_to(norm, (dens, patch))

    def flip_kernel(in_ref, out_ref):
        for at in range(0, in_ref.shape[0], patch):
            out_ref[:, at : at + patch] = in_ref[at : at + patch, :].T

    def flip_far_kernel(in_ref, out_ref):
        for block in range(blocks):
            for at in range(0, in_ref.shape[2], patch):
                out_ref[block, at : at + patch, :] = in_ref[block, :, at : at + patch].T

    def flip(kernel, x, shape):
        (out,) = call(kernel, [(shape, BF16)], [x], keep=(0,))
        return out

    def coefficients(grad, bound_ref, v_ref, out_ref):
        half = grad.astype(BF16)
        for i in range(0, rows, 2):
            both = dot_nn(half, v_ref[:, i * wide : (i + 2) * wide])
            for k in range(2):
                part = jnp.where(
                    kept_lanes(bound_ref, i + k), both[:, k * wide : (k + 1) * wide], 0.0
                )
                total = part[0:dens]
                for j in range(1, cols):
                    total = total + part[j * dens : (j + 1) * dens]
                out_ref[i + k, :, 0:wide] = total.astype(BF16)

    def norm_of(grad):
        line = jnp.sum(grad * grad, axis=1, keepdims=True)
        total = line[0:dens]
        for j in range(1, line.shape[0] // dens):
            total = total + line[j * dens : (j + 1) * dens]
        return total

    def coef_kernel(p0_ref, p2_ref, p4_ref, p6_ref, bound_ref, v_ref, out_ref, grad_ref):
        grad = (p0_ref[...].astype(F32) + p2_ref[...].astype(F32)) + (
            p4_ref[...].astype(F32) + p6_ref[...].astype(F32)
        )
        grad_ref[...] = grad
        coefficients(grad, bound_ref, v_ref, out_ref)
        mine = spread(norm_of(grad))
        for i in range(rows):
            out_ref[i, :, wide : wide + 128] = mine

    def image_of(in_ref, u_ref):
        left = jnp.concatenate([in_ref[c, :, 0:wide] for c in range(peers)], axis=1)
        return dot_nn(left, u_ref[...])

    def image_back_kernel(in_ref, u_ref, ut_ref, image_ref, gsq_ref, out_ref):
        image = image_of(in_ref, u_ref)
        image_ref[...] = image
        gsq_ref[...] = jnp.broadcast_to(
            jnp.sum(gather_sum(in_ref, wide, 128), axis=1, keepdims=True), (dens, 128)
        )
        high = image.astype(BF16)
        low = (image - high.astype(F32)).astype(BF16)
        both = dot_nn(jnp.concatenate([high, low], axis=0), ut_ref[...])
        back = both[0:dens] + both[dens : 2 * dens]
        mine = spread(norm_of(image))
        for peer in range(peers):
            out_ref[peer, :, 0:wide] = back[:, peer * wide : (peer + 1) * wide].astype(BF16)
            out_ref[peer, :, wide : wide + 128] = mine

    far_low = wide + 128

    def coef_far_kernel(
        p0_ref, p2_ref, p4_ref, p6_ref, grad_ref, gsq_ref, bound_ref, v_ref, far_ref,
        out_ref, first_ref, second_ref, step_ref, even_ref,
    ):
        wave = (p0_ref[...].astype(F32) + p2_ref[...].astype(F32)) + (
            p4_ref[...].astype(F32) + p6_ref[...].astype(F32)
        )
        isq = jnp.sum(wave[tall : tall + dens, 0:128], axis=1, keepdims=True)
        step = gsq_ref[:, 0:1] / (isq + 1e-6)
        step_ref[...] = jnp.broadcast_to(step, (dens, 128))
        steps = jnp.concatenate([step] * cols, axis=0)
        first = steps * grad_ref[...]
        second = grad_ref[...] - steps * wave[0:tall]
        first_ref[...] = first
        second_ref[...] = second
        coefficients(second, bound_ref, v_ref, out_ref)
        mine = spread(norm_of(second))
        lines = [
            jnp.concatenate([x[j * dens : (j + 1) * dens] for j in range(cols)], axis=1)
            for x in (first, second)
        ]
        left = jnp.concatenate(lines, axis=0).astype(BF16)
        even = dot_nn(left, far_ref[0])
        odd = dot_nn(left, far_ref[1])
        even_ref[...] = jnp.concatenate([even[0:dens], even[dens : 2 * dens]], axis=1).astype(BF16)
        send = jnp.concatenate([odd[0:dens], odd[dens : 2 * dens]], axis=1).astype(BF16)
        for i in range(rows):
            out_ref[i, :, wide : wide + 128] = mine
            out_ref[i, :, far_low : far_low + 2 * patch] = send

    def image_last_kernel(in_ref, u_ref, image_ref, gsq_ref, out_ref):
        image = image_of(in_ref, u_ref)
        image_ref[...] = image
        gsq_ref[...] = jnp.broadcast_to(
            jnp.sum(gather_sum(in_ref, wide, 128), axis=1, keepdims=True), (dens, 128)
        )
        here = lax.broadcasted_iota(jnp.int32, (dens, 128), 0) == lax.broadcasted_iota(
            jnp.int32, (dens, 128), 1
        )
        line = jnp.sum(jnp.where(here, norm_of(image), 0.0), axis=0, keepdims=True)
        for peer in range(devices):
            out_ref[peer] = line

    def slot_kernel(target_ref, order_ref, slot_ref):
        row, col = lax.axis_index("row"), lax.axis_index("col")
        mine = [order_ref[lax.bitwise_xor(row, m) * peers + col] for m in range(n_row)]
        for source in range(peers):
            target = target_ref[row * blocks + 1, source]
            slot = jnp.int32(n_row)
            for m in range(n_row):
                slot = jnp.where(target == mine[m], m, slot)
            slot_ref[source] = slot

    def route_kernel(slot_ref, even_ref, in_ref, keep_ref, give_ref, sum_ref):
        sum_ref[...] = jnp.zeros_like(sum_ref)
        sum_ref[n_row // 2] = even_ref[...].astype(F32) * jnp.where(
            lax.axis_index("col") % 2 == 0, 1.0, 0.0
        )
        for source in range(peers):
            slot = slot_ref[source]

            @pl.when(slot < n_row)
            def _():
                piece = in_ref[source, :, far_low : far_low + 2 * patch].astype(F32)
                sum_ref[slot] = sum_ref[slot] + piece

        for m in range(n_row):
            out_ref = keep_ref if m % 2 == 0 else give_ref
            out_ref[m // 2] = sum_ref[m].astype(BF16)

    def pair_kernel(own_ref, other_ref, out_ref):
        out_ref[0:tall, :] = (own_ref[0:tall] + other_ref[0:tall]).astype(BF16)
        low = slice(tall, tall + dens)
        out_ref[low, 0:128] = spread(own_ref[low, 0:1] + other_ref[low, 0:1])
        out_ref[low, 128:patch] = jnp.zeros((dens, patch - 128), BF16)

    def finish_kernel(
        norm_ref, gsq_ref, first_ref, second_ref, res_ref, image1_ref, image2_ref, step_ref,
        f0_ref, f2_ref, f4_ref, f6_ref, side_ref, dens_ref, out_res_ref, out_far_ref,
    ):
        line = norm_ref[0]
        for source in range(1, devices):
            line = line + norm_ref[source]
        here = lax.broadcasted_iota(jnp.int32, (dens, 128), 0) == lax.broadcasted_iota(
            jnp.int32, (dens, 128), 1
        )
        isq = jnp.sum(jnp.where(here, line, 0.0), axis=1, keepdims=True)
        step = gsq_ref[:, 0:1] / (isq + 1e-6)
        for j in range(cols):
            at = slice(j * dens, (j + 1) * dens)
            dens_ref[:, j * patch : (j + 1) * patch] = first_ref[at] + step * second_ref[at]
        out_res_ref[...] = (
            res_ref[...] - step_ref[:, 0:1] * image1_ref[...] - step * image2_ref[...]
        )
        both = side_ref[...].astype(F32) * jnp.where(lax.axis_index("col") % 2 == 0, 1.0, 0.0)
        for ref in (f0_ref, f2_ref, f4_ref, f6_ref):
            both = both + ref[...].astype(F32)
        field = both[:, 0:patch] + step * both[:, patch : 2 * patch]
        for d in range(dens):
            out_far_ref[:, d * patch : (d + 1) * patch] = field[d : d + 1]

    def row_shift(x, k):
        return lax.ppermute(x, "row", [(i, i ^ k) for i in range(n_row)])

    def hops(halves):
        arrived = []
        for k, half in zip((2, 4, 6), halves):
            arrived.append(row_shift(half, k))
        return arrived

    def over_rows(part):
        other = row_shift(part, 1)
        if part.shape[0] > tall:
            (half,) = call(pair_kernel, [(part.shape, BF16)], [part, other])
        else:
            half = (part + other).astype(BF16)
        half = lax.optimization_barrier(half)
        return [half] + hops([half] * 3)

    def over_col(x):
        return lax.all_to_all(x, "col", split_axis=0, concat_axis=0, tiled=True)

    left_scratch = (pltpu.VMEM((tall, rows * wide), BF16),)
    dma = pltpu.SemaphoreType.DMA
    sent, u_all, u_flip = call(
        back_kernel,
        [((peers, dens, wide), BF16), (u_flat.shape, BF16), (u_flat.shape[::-1], BF16)],
        [pltpu.with_memory_space_constraint(right_side, pltpu.HBM), u_flat],
        hbm=(0, 1),
        keep=(1, 2),
        scratch=(pltpu.VMEM((dens, patch), F32), dma((parts + 1,))),
    )
    sent, v_flat = lax.optimization_barrier((sent, v_factors.reshape(rows * wide, patch)))
    v_all = pltpu.with_memory_space_constraint(v_flat, pltpu.VMEM)
    landed, known = lax.optimization_barrier((over_col(sent), ranks))
    bound = jnp.repeat(known.T, dens, axis=0)
    (part,) = call(
        grad_kernel, [((tall, patch), F32)], [landed, bound, v_all], scratch=left_scratch
    )
    part, v_now, *tables = lax.optimization_barrier((part, v_all, block_target, recv_order))
    v_flip = flip(flip_kernel, v_now, (patch, v_now.shape[0]))
    (slot,) = call(slot_kernel, [((peers,), jnp.int32)], tables, smem=(0, 1), smem_out=True)
    *arrived, v_flip, slot = lax.optimization_barrier((*over_rows(part), v_flip, slot))
    sent, grad = call(
        coef_kernel,
        [((rows, dens, wide + 128), BF16), ((tall, patch), F32)],
        arrived + [bound, v_flip],
    )
    image1, gsq1, sent = call(
        image_back_kernel,
        [((dens, patch), F32), ((dens, 128), F32), ((peers, dens, wide + 128), BF16)],
        [over_col(sent), u_all, u_flip],
    )
    (part,) = call(
        grad_norm_kernel,
        [((tall + dens, patch), F32)],
        [over_col(sent), bound, v_all],
        scratch=left_scratch,
    )
    part, far_now = lax.optimization_barrier((part, far_all))
    far_flip = flip(flip_far_kernel, far_now, (blocks, far_now.shape[2], patch))
    *arrived, far_flip = lax.optimization_barrier((*over_rows(part), far_flip))
    sent, first, second, step1, even = call(
        coef_far_kernel,
        [
            ((rows, dens, far_low + 2 * patch), BF16),
            ((tall, patch), F32),
            ((tall, patch), F32),
            ((dens, 128), F32),
            ((dens, 2 * patch), BF16),
        ],
        arrived + [grad, gsq1, bound, v_flip, far_flip],
    )
    landed = over_col(sent)
    image2, gsq2, sent = call(
        image_last_kernel,
        [((dens, patch), F32), ((dens, 128), F32), ((devices, 1, 128), F32)],
        [landed, u_all],
    )
    norms = lax.all_to_all(sent, ("row", "col"), split_axis=0, concat_axis=0, tiled=True)
    keep, give = call(
        route_kernel,
        [((n_row // 2, dens, 2 * patch), BF16)] * 2,
        [slot, even, landed],
        smem=(0,),
        scratch=(pltpu.VMEM((n_row, dens, 2 * patch), F32),),
    )
    near = keep + row_shift(give, 1)
    pieces = [near[0]] + hops([near[k] for k in range(1, n_row // 2)])
    side = lax.ppermute(even, "col", [(c, c ^ 1) for c in range(peers)])
    densities, residual, far_field = call(
        finish_kernel,
        [((dens, cols * patch), F32), ((dens, patch), F32), ((1, dens * patch), F32)],
        [norms, gsq2, first, second, right_side, image1, image2, step1] + pieces + [side],
    )
    return densities, residual, far_field


def solution(mesh):
    return jax.shard_map(
        per_device,
        mesh=mesh,
        in_specs=(
            P(None, ("row", "col")),
            P(("row", "col"), None, None, None),
            P("row", "col", None, None),
            P("row", "col"),
            P("row", None, "col"),
            P(),
            P(),
        ),
        out_specs=(P(None, "col"), P(None, ("row", "col")), P(("row", "col"), None)),
        check_vma=False,
    )
```

```python
import jax
import jax.numpy as jnp
from jax import lax
from jax.experimental import pallas as pl
from jax.experimental.pallas import tpu as pltpu
from jax.sharding import PartitionSpec as P


F32, BF16 = jnp.float32, jnp.bfloat16
MIB = 1 << 20


def dot_nn(a, b):
    return lax.dot_general(a, b, (((1,), (0,)), ((), ())), preferred_element_type=F32)


def spread(value):
    high = value.astype(BF16).astype(F32)
    rest = value - high
    mid = rest.astype(BF16).astype(F32)
    low = rest - mid
    lane = lax.broadcasted_iota(jnp.int32, (value.shape[0], 128), 1)
    zero = jnp.zeros((value.shape[0], 128), F32)
    return jnp.where(
        lane == 0, high, jnp.where(lane == 1, mid, jnp.where(lane == 2, low, zero))
    ).astype(BF16)


def gather_sum(ref, low, width):
    total = ref[0, :, low : low + width].astype(F32)
    for source in range(1, ref.shape[0]):
        total = total + ref[source, :, low : low + width].astype(F32)
    return total


def call(kernel, outs, args, smem=(), hbm=(), keep=(), scratch=(), limit=8, smem_out=False, hbm_out=()):
    vm = pl.BlockSpec(memory_space=pltpu.VMEM)
    sm = pl.BlockSpec(memory_space=pltpu.SMEM)
    far_away = pl.BlockSpec(memory_space=pltpu.HBM)
    return pl.pallas_call(
        kernel,
        out_shape=tuple(
            pltpu.VMEM(s, d) if at in keep else jax.ShapeDtypeStruct(s, d)
            for at, (s, d) in enumerate(outs)
        ),
        in_specs=[
            sm if at in smem else far_away if at in hbm else vm for at in range(len(args))
        ],
        out_specs=tuple(
            sm if smem_out else far_away if at in hbm_out else vm for at in range(len(outs))
        ),
        scratch_shapes=list(scratch),
        compiler_params=pltpu.CompilerParams(vmem_limit_bytes=limit * MIB),
    )(*args)


def per_device(right_side, u_factors, v_factors, ranks, far_blocks, block_target, recv_order):
    dens = right_side.shape[0]
    all_cols, slots, patch = u_factors.shape[1:]
    rows, cols = v_factors.shape[:2]
    peers = all_cols // cols
    wide = cols * slots
    n_row = lax.axis_size("row")
    devices = n_row * peers
    tall = cols * dens
    blocks = far_blocks.shape[0]

    u_flat = pltpu.with_memory_space_constraint(
        u_factors.reshape(all_cols * slots, patch), pltpu.HBM
    )
    far_all = pltpu.with_memory_space_constraint(far_blocks, pltpu.VMEM)
    parts = 4

    def kept_lanes(bound_ref, row_patch):
        lane = lax.broadcasted_iota(jnp.int32, (tall, wide), 1)
        first = lax.broadcasted_iota(jnp.int32, (tall, wide), 0) // dens * slots
        at = lane - first
        return (at >= 0) & (at < bound_ref[:, row_patch : row_patch + 1])

    def back_kernel(res_hbm, u_hbm, out_ref, u_ref, ut_ref, res_ref, sems):
        share = u_flat.shape[0] // parts
        each = peers // parts
        copies = [pltpu.make_async_copy(res_hbm, res_ref, sems.at[parts])]
        for part in range(parts):
            at = pl.ds(part * share, share)
            copies.append(pltpu.make_async_copy(u_hbm.at[at], u_ref.at[at], sems.at[part]))
        for copy in copies:
            copy.start()
        copies[0].wait()
        half = res_ref[...].astype(BF16)
        for part in range(parts):
            copies[part + 1].wait()
            turned = u_ref[part * share : (part + 1) * share, :].T
            ut_ref[:, part * share : (part + 1) * share] = turned
            back = dot_nn(half, turned)
            for k in range(each):
                out_ref[part * each + k] = back[:, k * wide : (k + 1) * wide].astype(BF16)

    def fill_left(in_ref, bound_ref, left_ref):
        for i in range(rows):
            piece = in_ref[i, :, 0:wide].astype(F32)
            stacked = jnp.concatenate([piece] * cols, axis=0)
            left_ref[:, i * wide : (i + 1) * wide] = jnp.where(
                kept_lanes(bound_ref, i), stacked, 0.0
            ).astype(BF16)

    def grad_kernel(in_ref, bound_ref, v_ref, out_ref, left_ref):
        fill_left(in_ref, bound_ref, left_ref)
        out_ref[...] = dot_nn(left_ref[...], v_ref[...])

    def grad_norm_kernel(in_ref, bound_ref, v_ref, out_ref, left_ref):
        fill_left(in_ref, bound_ref, left_ref)
        out_ref[0:tall, :] = dot_nn(left_ref[...], v_ref[...])
        norm = jnp.sum(gather_sum(in_ref, wide, 128), axis=1, keepdims=True)
        out_ref[tall : tall + dens, :] = jnp.broadcast_to(norm, (dens, patch))

    def flip_kernel(in_ref, out_ref):
        for at in range(0, in_ref.shape[0], patch):
            out_ref[:, at : at + patch] = in_ref[at : at + patch, :].T

    def flip_far_kernel(in_ref, out_ref):
        for block in range(blocks):
            for at in range(0, in_ref.shape[2], patch):
                out_ref[block, at : at + patch, :] = in_ref[block, :, at : at + patch].T

    def flip(kernel, x, shape):
        (out,) = call(kernel, [(shape, BF16)], [x], keep=(0,))
        return out

    def coefficients(grad, bound_ref, v_ref, out_ref):
        half = grad.astype(BF16)
        for i in range(0, rows, 2):
            both = dot_nn(half, v_ref[:, i * wide : (i + 2) * wide])
            for k in range(2):
                part = jnp.where(
                    kept_lanes(bound_ref, i + k), both[:, k * wide : (k + 1) * wide], 0.0
                )
                total = part[0:dens]
                for j in range(1, cols):
                    total = total + part[j * dens : (j + 1) * dens]
                out_ref[i + k, :, 0:wide] = total.astype(BF16)

    def norm_of(grad):
        line = jnp.sum(grad * grad, axis=1, keepdims=True)
        total = line[0:dens]
        for j in range(1, line.shape[0] // dens):
            total = total + line[j * dens : (j + 1) * dens]
        return total

    def coef_kernel(p0_ref, p2_ref, p4_ref, p6_ref, bound_ref, v_ref, out_ref, grad_ref):
        grad = (p0_ref[...].astype(F32) + p2_ref[...].astype(F32)) + (
            p4_ref[...].astype(F32) + p6_ref[...].astype(F32)
        )
        grad_ref[...] = grad
        coefficients(grad, bound_ref, v_ref, out_ref)
        mine = spread(norm_of(grad))
        for i in range(rows):
            out_ref[i, :, wide : wide + 128] = mine

    def image_of(in_ref, u_ref):
        left = jnp.concatenate([in_ref[c, :, 0:wide] for c in range(peers)], axis=1)
        return dot_nn(left, u_ref[...])

    def image_back_kernel(in_ref, u_ref, ut_ref, image_ref, gsq_ref, out_ref):
        image = image_of(in_ref, u_ref)
        image_ref[...] = image
        gsq_ref[...] = jnp.broadcast_to(
            jnp.sum(gather_sum(in_ref, wide, 128), axis=1, keepdims=True), (dens, 128)
        )
        high = image.astype(BF16)
        low = (image - high.astype(F32)).astype(BF16)
        both = dot_nn(jnp.concatenate([high, low], axis=0), ut_ref[...])
        back = both[0:dens] + both[dens : 2 * dens]
        mine = spread(norm_of(image))
        for peer in range(peers):
            out_ref[peer, :, 0:wide] = back[:, peer * wide : (peer + 1) * wide].astype(BF16)
            out_ref[peer, :, wide : wide + 128] = mine

    far_low = wide + 128

    def coef_far_kernel(
        p0_ref, p2_ref, p4_ref, p6_ref, grad_ref, gsq_ref, bound_ref, v_ref, far_ref,
        out_ref, first_ref, second_ref, step_ref, even_ref,
    ):
        wave = (p0_ref[...].astype(F32) + p2_ref[...].astype(F32)) + (
            p4_ref[...].astype(F32) + p6_ref[...].astype(F32)
        )
        isq = jnp.sum(wave[tall : tall + dens, 0:128], axis=1, keepdims=True)
        step = gsq_ref[:, 0:1] / (isq + 1e-6)
        step_ref[...] = jnp.broadcast_to(step, (dens, 128))
        steps = jnp.concatenate([step] * cols, axis=0)
        first = steps * grad_ref[...]
        second = grad_ref[...] - steps * wave[0:tall]
        first_ref[...] = first
        second_ref[...] = second
        coefficients(second, bound_ref, v_ref, out_ref)
        mine = spread(norm_of(second))
        lines = [
            jnp.concatenate([x[j * dens : (j + 1) * dens] for j in range(cols)], axis=1)
            for x in (first, second)
        ]
        left = jnp.concatenate(lines, axis=0).astype(BF16)
        even = dot_nn(left, far_ref[0])
        odd = dot_nn(left, far_ref[1])
        even_ref[...] = jnp.concatenate([even[0:dens], even[dens : 2 * dens]], axis=1).astype(BF16)
        send = jnp.concatenate([odd[0:dens], odd[dens : 2 * dens]], axis=1).astype(BF16)
        for i in range(rows):
            out_ref[i, :, wide : wide + 128] = mine
            out_ref[i, :, far_low : far_low + 2 * patch] = send

    def slot_kernel(target_ref, order_ref, slot_ref):
        row, col = lax.axis_index("row"), lax.axis_index("col")
        mine = [order_ref[lax.bitwise_xor(row, m) * peers + col] for m in range(n_row)]
        for source in range(peers):
            target = target_ref[row * blocks + 1, source]
            slot = jnp.int32(n_row)
            for m in range(n_row):
                slot = jnp.where(target == mine[m], m, slot)
            slot_ref[source] = slot

    def image_last_kernel(
        slot_ref, even_ref, in_ref, u_ref, image_ref, gsq_ref, out_hbm, keep_ref, give_ref,
        sum_ref, out_ref, sem,
    ):
        image = image_of(in_ref, u_ref)
        image_ref[...] = image
        gsq_ref[...] = jnp.broadcast_to(
            jnp.sum(gather_sum(in_ref, wide, 128), axis=1, keepdims=True), (dens, 128)
        )
        here = lax.broadcasted_iota(jnp.int32, (dens, 128), 0) == lax.broadcasted_iota(
            jnp.int32, (dens, 128), 1
        )
        line = jnp.sum(jnp.where(here, norm_of(image), 0.0), axis=0, keepdims=True)
        for peer in range(devices):
            out_ref[peer] = line
        leave = pltpu.make_async_copy(out_ref, out_hbm, sem)
        leave.start()
        sum_ref[...] = jnp.zeros_like(sum_ref)
        sum_ref[n_row // 2] = even_ref[...].astype(F32) * jnp.where(
            lax.axis_index("col") % 2 == 0, 1.0, 0.0
        )
        for source in range(peers):
            slot = slot_ref[source]

            @pl.when(slot < n_row)
            def _():
                piece = in_ref[source, :, far_low : far_low + 2 * patch].astype(F32)
                sum_ref[slot] = sum_ref[slot] + piece

        for m in range(n_row):
            to_ref = keep_ref if m % 2 == 0 else give_ref
            to_ref[m // 2] = sum_ref[m].astype(BF16)
        leave.wait()

    def pair_kernel(own_ref, other_ref, out_ref):
        out_ref[0:tall, :] = (own_ref[0:tall] + other_ref[0:tall]).astype(BF16)
        low = slice(tall, tall + dens)
        out_ref[low, 0:128] = spread(own_ref[low, 0:1] + other_ref[low, 0:1])
        out_ref[low, 128:patch] = jnp.zeros((dens, patch - 128), BF16)

    def finish_kernel(
        norm_ref, gsq_ref, first_ref, second_ref, res_ref, image1_ref, image2_ref, step_ref,
        f0_ref, f2_ref, f4_ref, f6_ref, side_ref, dens_ref, out_res_ref, out_far_ref,
    ):
        line = norm_ref[0]
        for source in range(1, devices):
            line = line + norm_ref[source]
        here = lax.broadcasted_iota(jnp.int32, (dens, 128), 0) == lax.broadcasted_iota(
            jnp.int32, (dens, 128), 1
        )
        isq = jnp.sum(jnp.where(here, line, 0.0), axis=1, keepdims=True)
        step = gsq_ref[:, 0:1] / (isq + 1e-6)
        for j in range(cols):
            at = slice(j * dens, (j + 1) * dens)
            dens_ref[:, j * patch : (j + 1) * patch] = first_ref[at] + step * second_ref[at]
        out_res_ref[...] = (
            res_ref[...] - step_ref[:, 0:1] * image1_ref[...] - step * image2_ref[...]
        )
        both = side_ref[...].astype(F32) * jnp.where(lax.axis_index("col") % 2 == 0, 1.0, 0.0)
        for ref in (f0_ref, f2_ref, f4_ref, f6_ref):
            both = both + ref[...].astype(F32)
        field = both[:, 0:patch] + step * both[:, patch : 2 * patch]
        for d in range(dens):
            out_far_ref[:, d * patch : (d + 1) * patch] = field[d : d + 1]

    def row_shift(x, k):
        return lax.ppermute(x, "row", [(i, i ^ k) for i in range(n_row)])

    def hops(halves):
        arrived = []
        for k, half in zip((2, 4, 6), halves):
            arrived.append(row_shift(half, k))
        return arrived

    def over_rows(part):
        other = row_shift(part, 1)
        if part.shape[0] > tall:
            (half,) = call(pair_kernel, [(part.shape, BF16)], [part, other])
        else:
            half = (part + other).astype(BF16)
        half = lax.optimization_barrier(half)
        return [half] + hops([half] * 3)

    def over_col(x):
        return lax.all_to_all(x, "col", split_axis=0, concat_axis=0, tiled=True)

    left_scratch = (pltpu.VMEM((tall, rows * wide), BF16),)
    dma = pltpu.SemaphoreType.DMA
    sent, u_all, u_flip = call(
        back_kernel,
        [((peers, dens, wide), BF16), (u_flat.shape, BF16), (u_flat.shape[::-1], BF16)],
        [pltpu.with_memory_space_constraint(right_side, pltpu.HBM), u_flat],
        hbm=(0, 1),
        keep=(1, 2),
        scratch=(pltpu.VMEM((dens, patch), F32), dma((parts + 1,))),
    )
    sent, v_flat = lax.optimization_barrier((sent, v_factors.reshape(rows * wide, patch)))
    v_all = pltpu.with_memory_space_constraint(v_flat, pltpu.VMEM)
    landed, known = lax.optimization_barrier((over_col(sent), ranks))
    bound = jnp.repeat(known.T, dens, axis=0)
    (part,) = call(
        grad_kernel, [((tall, patch), F32)], [landed, bound, v_all], scratch=left_scratch
    )
    part, v_now, *tables = lax.optimization_barrier((part, v_all, block_target, recv_order))
    v_flip = flip(flip_kernel, v_now, (patch, v_now.shape[0]))
    (slot,) = call(slot_kernel, [((peers,), jnp.int32)], tables, smem=(0, 1), smem_out=True)
    *arrived, v_flip, slot = lax.optimization_barrier((*over_rows(part), v_flip, slot))
    sent, grad = call(
        coef_kernel,
        [((rows, dens, wide + 128), BF16), ((tall, patch), F32)],
        arrived + [bound, v_flip],
    )
    image1, gsq1, sent = call(
        image_back_kernel,
        [((dens, patch), F32), ((dens, 128), F32), ((peers, dens, wide + 128), BF16)],
        [over_col(sent), u_all, u_flip],
    )
    (part,) = call(
        grad_norm_kernel,
        [((tall + dens, patch), F32)],
        [over_col(sent), bound, v_all],
        scratch=left_scratch,
    )
    part, far_now = lax.optimization_barrier((part, far_all))
    far_flip = flip(flip_far_kernel, far_now, (blocks, far_now.shape[2], patch))
    *arrived, far_flip = lax.optimization_barrier((*over_rows(part), far_flip))
    sent, first, second, step1, even = call(
        coef_far_kernel,
        [
            ((rows, dens, far_low + 2 * patch), BF16),
            ((tall, patch), F32),
            ((tall, patch), F32),
            ((dens, 128), F32),
            ((dens, 2 * patch), BF16),
        ],
        arrived + [grad, gsq1, bound, v_flip, far_flip],
    )
    landed = over_col(sent)
    image2, gsq2, sent, keep, give = call(
        image_last_kernel,
        [((dens, patch), F32), ((dens, 128), F32), ((devices, 1, 128), F32)]
        + [((n_row // 2, dens, 2 * patch), BF16)] * 2,
        [slot, even, landed, u_all],
        smem=(0,),
        hbm_out=(2,),
        scratch=(
            pltpu.VMEM((n_row, dens, 2 * patch), F32),
            pltpu.VMEM((devices, 1, 128), F32),
            dma(()),
        ),
    )
    norms = lax.all_to_all(sent, ("row", "col"), split_axis=0, concat_axis=0, tiled=True)
    near = keep + row_shift(give, 1)
    pieces = [near[0]] + hops([near[k] for k in range(1, n_row // 2)])
    side = lax.ppermute(even, "col", [(c, c ^ 1) for c in range(peers)])
    densities, residual, far_field = call(
        finish_kernel,
        [((dens, cols * patch), F32), ((dens, patch), F32), ((1, dens * patch), F32)],
        [norms, gsq2, first, second, right_side, image1, image2, step1] + pieces + [side],
    )
    return densities, residual, far_field


def solution(mesh):
    return jax.shard_map(
        per_device,
        mesh=mesh,
        in_specs=(
            P(None, ("row", "col")),
            P(("row", "col"), None, None, None),
            P("row", "col", None, None),
            P("row", "col"),
            P("row", None, "col"),
            P(),
            P(),
        ),
        out_specs=(P(None, "col"), P(None, ("row", "col")), P(("row", "col"), None)),
        check_vma=False,
    )
```

```python
import jax
import jax.numpy as jnp
from jax import lax
from jax.experimental import pallas as pl
from jax.experimental.pallas import tpu as pltpu
from jax.sharding import PartitionSpec as P


F32, BF16 = jnp.float32, jnp.bfloat16
MIB = 1 << 20


def dot_nn(a, b):
    return lax.dot_general(a, b, (((1,), (0,)), ((), ())), preferred_element_type=F32)


def spread(value):
    high = value.astype(BF16).astype(F32)
    rest = value - high
    mid = rest.astype(BF16).astype(F32)
    low = rest - mid
    lane = lax.broadcasted_iota(jnp.int32, (value.shape[0], 128), 1)
    zero = jnp.zeros((value.shape[0], 128), F32)
    return jnp.where(
        lane == 0, high, jnp.where(lane == 1, mid, jnp.where(lane == 2, low, zero))
    ).astype(BF16)


def gather_sum(ref, low, width):
    total = ref[0, :, low : low + width].astype(F32)
    for source in range(1, ref.shape[0]):
        total = total + ref[source, :, low : low + width].astype(F32)
    return total


def call(kernel, outs, args, smem=(), hbm=(), keep=(), scratch=(), limit=8, smem_out=False, hbm_out=()):
    vm = pl.BlockSpec(memory_space=pltpu.VMEM)
    sm = pl.BlockSpec(memory_space=pltpu.SMEM)
    far_away = pl.BlockSpec(memory_space=pltpu.HBM)
    return pl.pallas_call(
        kernel,
        out_shape=tuple(
            pltpu.VMEM(s, d) if at in keep else jax.ShapeDtypeStruct(s, d)
            for at, (s, d) in enumerate(outs)
        ),
        in_specs=[
            sm if at in smem else far_away if at in hbm else vm for at in range(len(args))
        ],
        out_specs=tuple(
            sm if smem_out else far_away if at in hbm_out else vm for at in range(len(outs))
        ),
        scratch_shapes=list(scratch),
        compiler_params=pltpu.CompilerParams(vmem_limit_bytes=limit * MIB),
    )(*args)


def per_device(right_side, u_factors, v_factors, ranks, far_blocks, block_target, recv_order):
    dens = right_side.shape[0]
    all_cols, slots, patch = u_factors.shape[1:]
    rows, cols = v_factors.shape[:2]
    peers = all_cols // cols
    wide = cols * slots
    n_row = lax.axis_size("row")
    devices = n_row * peers
    tall = cols * dens
    blocks = far_blocks.shape[0]

    u_flat = pltpu.with_memory_space_constraint(
        u_factors.reshape(all_cols * slots, patch), pltpu.HBM
    )
    far_all = pltpu.with_memory_space_constraint(far_blocks, pltpu.VMEM)
    parts = 4

    def kept_lanes(bound_ref, row_patch):
        lane = lax.broadcasted_iota(jnp.int32, (tall, wide), 1)
        first = lax.broadcasted_iota(jnp.int32, (tall, wide), 0) // dens * slots
        at = lane - first
        return (at >= 0) & (at < bound_ref[:, row_patch : row_patch + 1])

    def back_kernel(res_hbm, u_hbm, out_ref, u_ref, ut_ref, res_ref, sems):
        share = u_flat.shape[0] // parts
        each = peers // parts
        copies = [pltpu.make_async_copy(res_hbm, res_ref, sems.at[parts])]
        for part in range(parts):
            at = pl.ds(part * share, share)
            copies.append(pltpu.make_async_copy(u_hbm.at[at], u_ref.at[at], sems.at[part]))
        for copy in copies:
            copy.start()
        copies[0].wait()
        half = res_ref[...].astype(BF16)
        for part in range(parts):
            copies[part + 1].wait()
            turned = u_ref[part * share : (part + 1) * share, :].T
            ut_ref[:, part * share : (part + 1) * share] = turned
            back = dot_nn(half, turned)
            for k in range(each):
                out_ref[part * each + k] = back[:, k * wide : (k + 1) * wide].astype(BF16)

    def fill_left(in_ref, bound_ref, left_ref):
        for i in range(rows):
            piece = in_ref[i, :, 0:wide].astype(F32)
            stacked = jnp.concatenate([piece] * cols, axis=0)
            left_ref[:, i * wide : (i + 1) * wide] = jnp.where(
                kept_lanes(bound_ref, i), stacked, 0.0
            ).astype(BF16)

    def grad_kernel(in_ref, bound_ref, v_ref, out_ref, left_ref):
        fill_left(in_ref, bound_ref, left_ref)
        out_ref[...] = dot_nn(left_ref[...], v_ref[...])

    def grad_norm_kernel(in_ref, bound_ref, v_ref, out_ref, left_ref):
        fill_left(in_ref, bound_ref, left_ref)
        out_ref[0:tall, :] = dot_nn(left_ref[...], v_ref[...])
        norm = jnp.sum(gather_sum(in_ref, wide, 128), axis=1, keepdims=True)
        out_ref[tall : tall + dens, :] = jnp.broadcast_to(norm, (dens, patch))

    def flip_kernel(in_ref, out_ref):
        for at in range(0, in_ref.shape[0], patch):
            out_ref[:, at : at + patch] = in_ref[at : at + patch, :].T

    def flip_far_kernel(in_ref, out_ref):
        for block in range(blocks):
            for at in range(0, in_ref.shape[2], patch):
                out_ref[block, at : at + patch, :] = in_ref[block, :, at : at + patch].T

    def flip(kernel, x, shape):
        (out,) = call(kernel, [(shape, BF16)], [x], keep=(0,))
        return out

    def coefficients(grad, bound_ref, v_ref, out_ref):
        half = grad.astype(BF16)
        for i in range(0, rows, 4):
            both = dot_nn(half, v_ref[:, i * wide : (i + 4) * wide])
            for k in range(4):
                part = jnp.where(
                    kept_lanes(bound_ref, i + k), both[:, k * wide : (k + 1) * wide], 0.0
                )
                total = part[0:dens]
                for j in range(1, cols):
                    total = total + part[j * dens : (j + 1) * dens]
                out_ref[i + k, :, 0:wide] = total.astype(BF16)

    def norm_of(grad):
        line = jnp.sum(grad * grad, axis=1, keepdims=True)
        total = line[0:dens]
        for j in range(1, line.shape[0] // dens):
            total = total + line[j * dens : (j + 1) * dens]
        return total

    def coef_kernel(p0_ref, p2_ref, p4_ref, p6_ref, bound_ref, v_ref, out_ref, grad_ref):
        grad = (p0_ref[...].astype(F32) + p2_ref[...].astype(F32)) + (
            p4_ref[...].astype(F32) + p6_ref[...].astype(F32)
        )
        grad_ref[...] = grad
        coefficients(grad, bound_ref, v_ref, out_ref)
        mine = spread(norm_of(grad))
        for i in range(rows):
            out_ref[i, :, wide : wide + 128] = mine

    def image_of(in_ref, u_ref):
        left = jnp.concatenate([in_ref[c, :, 0:wide] for c in range(peers)], axis=1)
        return dot_nn(left, u_ref[...])

    def image_back_kernel(in_ref, u_ref, ut_ref, image_ref, gsq_ref, out_ref):
        image = image_of(in_ref, u_ref)
        image_ref[...] = image
        gsq_ref[...] = jnp.broadcast_to(
            jnp.sum(gather_sum(in_ref, wide, 128), axis=1, keepdims=True), (dens, 128)
        )
        high = image.astype(BF16)
        low = (image - high.astype(F32)).astype(BF16)
        both = dot_nn(jnp.concatenate([high, low], axis=0), ut_ref[...])
        back = both[0:dens] + both[dens : 2 * dens]
        mine = spread(norm_of(image))
        for peer in range(peers):
            out_ref[peer, :, 0:wide] = back[:, peer * wide : (peer + 1) * wide].astype(BF16)
            out_ref[peer, :, wide : wide + 128] = mine

    far_low = wide + 128

    def coef_far_kernel(
        p0_ref, p2_ref, p4_ref, p6_ref, grad_ref, gsq_ref, bound_ref, v_ref, far_ref,
        out_ref, first_ref, second_ref, step_ref, even_ref,
    ):
        wave = (p0_ref[...].astype(F32) + p2_ref[...].astype(F32)) + (
            p4_ref[...].astype(F32) + p6_ref[...].astype(F32)
        )
        isq = jnp.sum(wave[tall : tall + dens, 0:128], axis=1, keepdims=True)
        step = gsq_ref[:, 0:1] / (isq + 1e-6)
        step_ref[...] = jnp.broadcast_to(step, (dens, 128))
        steps = jnp.concatenate([step] * cols, axis=0)
        first = steps * grad_ref[...]
        second = grad_ref[...] - steps * wave[0:tall]
        first_ref[...] = first
        second_ref[...] = second
        coefficients(second, bound_ref, v_ref, out_ref)
        mine = spread(norm_of(second))
        lines = [
            jnp.concatenate([x[j * dens : (j + 1) * dens] for j in range(cols)], axis=1)
            for x in (first, second)
        ]
        left = jnp.concatenate(lines, axis=0).astype(BF16)
        even = dot_nn(left, far_ref[0])
        odd = dot_nn(left, far_ref[1])
        even_ref[...] = jnp.concatenate([even[0:dens], even[dens : 2 * dens]], axis=1).astype(BF16)
        send = jnp.concatenate([odd[0:dens], odd[dens : 2 * dens]], axis=1).astype(BF16)
        for i in range(rows):
            out_ref[i, :, wide : wide + 128] = mine
            out_ref[i, :, far_low : far_low + 2 * patch] = send

    def slot_kernel(target_ref, order_ref, slot_ref):
        row, col = lax.axis_index("row"), lax.axis_index("col")
        mine = [order_ref[lax.bitwise_xor(row, m) * peers + col] for m in range(n_row)]
        for source in range(peers):
            target = target_ref[row * blocks + 1, source]
            slot = jnp.int32(n_row)
            for m in range(n_row):
                slot = jnp.where(target == mine[m], m, slot)
            slot_ref[source] = slot

    def image_last_kernel(
        slot_ref, even_ref, in_ref, u_ref, image_ref, gsq_ref, out_hbm, keep_ref, give_ref,
        sum_ref, out_ref, sem,
    ):
        image = image_of(in_ref, u_ref)
        image_ref[...] = image
        gsq_ref[...] = jnp.broadcast_to(
            jnp.sum(gather_sum(in_ref, wide, 128), axis=1, keepdims=True), (dens, 128)
        )
        here = lax.broadcasted_iota(jnp.int32, (dens, 128), 0) == lax.broadcasted_iota(
            jnp.int32, (dens, 128), 1
        )
        line = jnp.sum(jnp.where(here, norm_of(image), 0.0), axis=0, keepdims=True)
        for peer in range(devices):
            out_ref[peer] = line
        leave = pltpu.make_async_copy(out_ref, out_hbm, sem)
        leave.start()
        sum_ref[...] = jnp.zeros_like(sum_ref)
        sum_ref[n_row // 2] = even_ref[...].astype(F32) * jnp.where(
            lax.axis_index("col") % 2 == 0, 1.0, 0.0
        )
        for source in range(peers):
            slot = slot_ref[source]

            @pl.when(slot < n_row)
            def _():
                piece = in_ref[source, :, far_low : far_low + 2 * patch].astype(F32)
                sum_ref[slot] = sum_ref[slot] + piece

        for m in range(n_row):
            to_ref = keep_ref if m % 2 == 0 else give_ref
            to_ref[m // 2] = sum_ref[m].astype(BF16)
        leave.wait()

    def pair_kernel(own_ref, other_ref, out_ref):
        out_ref[0:tall, :] = (own_ref[0:tall] + other_ref[0:tall]).astype(BF16)
        low = slice(tall, tall + dens)
        out_ref[low, 0:128] = spread(own_ref[low, 0:1] + other_ref[low, 0:1])
        out_ref[low, 128:patch] = jnp.zeros((dens, patch - 128), BF16)

    def finish_kernel(
        norm_ref, gsq_ref, first_ref, second_ref, res_ref, image1_ref, image2_ref, step_ref,
        f0_ref, f2_ref, f4_ref, f6_ref, side_ref, dens_ref, out_res_ref, out_far_ref,
    ):
        line = norm_ref[0]
        for source in range(1, devices):
            line = line + norm_ref[source]
        here = lax.broadcasted_iota(jnp.int32, (dens, 128), 0) == lax.broadcasted_iota(
            jnp.int32, (dens, 128), 1
        )
        isq = jnp.sum(jnp.where(here, line, 0.0), axis=1, keepdims=True)
        step = gsq_ref[:, 0:1] / (isq + 1e-6)
        for j in range(cols):
            at = slice(j * dens, (j + 1) * dens)
            dens_ref[:, j * patch : (j + 1) * patch] = first_ref[at] + step * second_ref[at]
        out_res_ref[...] = (
            res_ref[...] - step_ref[:, 0:1] * image1_ref[...] - step * image2_ref[...]
        )
        both = side_ref[...].astype(F32) * jnp.where(lax.axis_index("col") % 2 == 0, 1.0, 0.0)
        for ref in (f0_ref, f2_ref, f4_ref, f6_ref):
            both = both + ref[...].astype(F32)
        field = both[:, 0:patch] + step * both[:, patch : 2 * patch]
        for d in range(dens):
            out_far_ref[:, d * patch : (d + 1) * patch] = field[d : d + 1]

    def row_shift(x, k):
        return lax.ppermute(x, "row", [(i, i ^ k) for i in range(n_row)])

    def hops(halves):
        arrived = []
        for k, half in zip((2, 4, 6), halves):
            arrived.append(row_shift(half, k))
        return arrived

    def over_rows(part):
        other = row_shift(part, 1)
        if part.shape[0] > tall:
            (half,) = call(pair_kernel, [(part.shape, BF16)], [part, other])
        else:
            half = (part + other).astype(BF16)
        half = lax.optimization_barrier(half)
        return [half] + hops([half] * 3)

    def over_col(x):
        return lax.all_to_all(x, "col", split_axis=0, concat_axis=0, tiled=True)

    left_scratch = (pltpu.VMEM((tall, rows * wide), BF16),)
    dma = pltpu.SemaphoreType.DMA
    sent, u_all, u_flip = call(
        back_kernel,
        [((peers, dens, wide), BF16), (u_flat.shape, BF16), (u_flat.shape[::-1], BF16)],
        [pltpu.with_memory_space_constraint(right_side, pltpu.HBM), u_flat],
        hbm=(0, 1),
        keep=(1, 2),
        scratch=(pltpu.VMEM((dens, patch), F32), dma((parts + 1,))),
    )
    sent, v_flat = lax.optimization_barrier((sent, v_factors.reshape(rows * wide, patch)))
    v_all = pltpu.with_memory_space_constraint(v_flat, pltpu.VMEM)
    landed, known = lax.optimization_barrier((over_col(sent), ranks))
    bound = jnp.repeat(known.T, dens, axis=0)
    (part,) = call(
        grad_kernel, [((tall, patch), F32)], [landed, bound, v_all], scratch=left_scratch
    )
    part, v_now, *tables = lax.optimization_barrier((part, v_all, block_target, recv_order))
    v_flip = flip(flip_kernel, v_now, (patch, v_now.shape[0]))
    (slot,) = call(slot_kernel, [((peers,), jnp.int32)], tables, smem=(0, 1), smem_out=True)
    *arrived, v_flip, slot = lax.optimization_barrier((*over_rows(part), v_flip, slot))
    sent, grad = call(
        coef_kernel,
        [((rows, dens, wide + 128), BF16), ((tall, patch), F32)],
        arrived + [bound, v_flip],
    )
    image1, gsq1, sent = call(
        image_back_kernel,
        [((dens, patch), F32), ((dens, 128), F32), ((peers, dens, wide + 128), BF16)],
        [over_col(sent), u_all, u_flip],
    )
    (part,) = call(
        grad_norm_kernel,
        [((tall + dens, patch), F32)],
        [over_col(sent), bound, v_all],
        scratch=left_scratch,
    )
    part, far_now = lax.optimization_barrier((part, far_all))
    far_flip = flip(flip_far_kernel, far_now, (blocks, far_now.shape[2], patch))
    *arrived, far_flip = lax.optimization_barrier((*over_rows(part), far_flip))
    sent, first, second, step1, even = call(
        coef_far_kernel,
        [
            ((rows, dens, far_low + 2 * patch), BF16),
            ((tall, patch), F32),
            ((tall, patch), F32),
            ((dens, 128), F32),
            ((dens, 2 * patch), BF16),
        ],
        arrived + [grad, gsq1, bound, v_flip, far_flip],
    )
    landed = over_col(sent)
    image2, gsq2, sent, keep, give = call(
        image_last_kernel,
        [((dens, patch), F32), ((dens, 128), F32), ((devices, 1, 128), F32)]
        + [((n_row // 2, dens, 2 * patch), BF16)] * 2,
        [slot, even, landed, u_all],
        smem=(0,),
        hbm_out=(2,),
        scratch=(
            pltpu.VMEM((n_row, dens, 2 * patch), F32),
            pltpu.VMEM((devices, 1, 128), F32),
            dma(()),
        ),
    )
    norms = lax.all_to_all(sent, ("row", "col"), split_axis=0, concat_axis=0, tiled=True)
    near = keep + row_shift(give, 1)
    pieces = [near[0]] + hops([near[k] for k in range(1, n_row // 2)])
    side = lax.ppermute(even, "col", [(c, c ^ 1) for c in range(peers)])
    densities, residual, far_field = call(
        finish_kernel,
        [((dens, cols * patch), F32), ((dens, patch), F32), ((1, dens * patch), F32)],
        [norms, gsq2, first, second, right_side, image1, image2, step1] + pieces + [side],
    )
    return densities, residual, far_field


def solution(mesh):
    return jax.shard_map(
        per_device,
        mesh=mesh,
        in_specs=(
            P(None, ("row", "col")),
            P(("row", "col"), None, None, None),
            P("row", "col", None, None),
            P("row", "col"),
            P("row", None, "col"),
            P(),
            P(),
        ),
        out_specs=(P(None, "col"), P(None, ("row", "col")), P(("row", "col"), None)),
        check_vma=False,
    )
```
